256 devices in a mesh: seq: 64 (over x, z, core), ch: 4 (over y).
Axes of the slice: x: 4, y: 4, z: 8, core: 2. Of those that a mesh axis runs over, the one named last changes fastest.
Arguments:
- gate_rows: bfloat16 [32768, 2048], P(('seq', 'ch')), may hold values from -6 to 6
- key_rows: bfloat16 [32768, 2048], P(('seq', 'ch')), may hold values from -6 to 6
- value_rows: bfloat16 [32768, 2048], P(('seq', 'ch')), may hold values from -6 to 6
- spectrum: float32 [2, 128, 512, 2048], P(None, 'seq', None, 'ch'), may hold values from -6 to 6
- skip_bias: float32 [2048], replicated, may hold values from -1 to 1
Outputs:
- gated: bfloat16 [32768, 2048], P(('seq', 'ch'))
The draws below stay inside these ranges and needn't reach their ends.
All inputs are finite; a program needn't handle non-finite values.
Results may differ from the reference program's by a relative error of at most 0.0049.
Values may be sent and summed in bfloat16 or wider, within the bound.
A program may use at most 128 MiB of HBM per device.

```python
import jax
import jax.numpy as jnp
from jax import lax

C = 2048
TOK_SEQ = 512
LENGTH = 32768
OFFSETS = 128


def shard_levels(key, dims, pieces, smallest, top_value):
    loudness = 1.0
    for axis_at, shards_of in pieces:
        heights = jax.random.uniform(jax.random.fold_in(jax.random.fold_in(key, 6), axis_at), (shards_of,), jnp.float32, smallest / len(pieces), top_value / len(pieces))
        loudness = loudness * jnp.repeat(jnp.exp(heights), dims[axis_at] // shards_of).reshape((-1,) + (1,) * (len(dims) - 1 - axis_at))
    return loudness


def scatter_about(stream_key, shape, scale, most, split=(), dtype=jnp.bfloat16):
    values = jax.random.normal(stream_key, shape, jnp.float32) * scale
    if len(split) > 0:
        values = shard_levels(stream_key, shape, split, -0.22, 0.18) * values
    return jnp.clip(values, min=-most, max=most).astype(dtype)


def setup_inputs(seed: int = 0) -> dict:
    arg_keys = jax.random.split(jax.random.key(seed), 6)
    gate_rows = scatter_about(arg_keys[0], (LENGTH, C), 1.0, 6.0, ((0, 256),))
    key_rows = scatter_about(arg_keys[1], (LENGTH, C), 1.0, 6.0, ((0, 256),))
    value_rows = scatter_about(arg_keys[2], (LENGTH, C), 1.0, 6.0, ((0, 256),))
    spectrum = scatter_about(arg_keys[3], (2, OFFSETS, TOK_SEQ, C), 1.0, 6.0, ((1, 64), (3, 4)), jnp.float32)
    skip_bias = jnp.clip(jax.random.uniform(arg_keys[4], (C,), jnp.float32, -1.0, 1.0), -1.0, 1.0)
    return dict(gate_rows=gate_rows, key_rows=key_rows, value_rows=value_rows, spectrum=spectrum, skip_bias=skip_bias)


def reference(gate_rows, key_rows, value_rows, spectrum, skip_bias):
    product = (key_rows.astype(jnp.float32) * value_rows.astype(jnp.float32)).astype(jnp.bfloat16)
    length_two = 2 * LENGTH
    spec_real = jnp.transpose(spectrum[0], (1, 0, 2)).reshape(length_two, C)
    spec_imag = jnp.transpose(spectrum[1], (1, 0, 2)).reshape(length_two, C)
    width = min(C, 128)
    count = C // width
    blocks_in = jnp.transpose(product.astype(jnp.float32).reshape(LENGTH, count, width), (1, 0, 2))
    blocks_re = jnp.transpose(spec_real.reshape(length_two, count, width), (1, 0, 2))
    blocks_im = jnp.transpose(spec_imag.reshape(length_two, count, width), (1, 0, 2))

    def one_block(items):
        signal, part_re, part_im = items
        transform = jnp.fft.fft(signal, n=length_two, axis=0)
        filtered = transform * (part_re + 1j * part_im)
        return jnp.real(jnp.fft.ifft(filtered, axis=0))[:LENGTH]

    fields = lax.map(one_block, (blocks_in, blocks_re, blocks_im))
    field = jnp.transpose(fields, (1, 0, 2)).reshape(LENGTH, C)
    gated = gate_rows.astype(jnp.float32) * (field + skip_bias[None, :] * product.astype(jnp.float32))
    return gated.astype(jnp.bfloat16)
```

```python
import math

import jax
import jax.numpy as jnp
import numpy as np
from jax import lax
from jax.sharding import PartitionSpec as P

f32, bf16 = jnp.float32, jnp.bfloat16


def phase_table(first, second, modulus):
    turns = first[:, None] * second[None, :] % modulus
    angles = turns.astype(f32) * (2.0 * math.pi / modulus)
    return (jnp.cos(angles), jnp.sin(angles))


def dot(eq, a, b):
    return jnp.einsum(eq, a.astype(bf16), b.astype(bf16), preferred_element_type=f32)


def convolve(product, spectrum):
    seq_count = lax.axis_size("seq")
    tokens, width = product.shape
    length_two = 2 * seq_count * tokens
    offsets = jnp.arange(2 * seq_count, dtype=jnp.int32)
    places = jnp.arange(seq_count, dtype=jnp.int32)
    residues = jnp.arange(tokens, dtype=jnp.int32)
    off_cos, off_sin = phase_table(offsets, places, 2 * seq_count)
    res_cos, res_sin = phase_table(residues, residues, tokens)
    block = tokens // seq_count
    device = lax.axis_index("seq")
    values = lax.all_to_all(product.reshape(1, tokens, width), "seq", split_axis=1, concat_axis=0, tiled=True)
    off = jnp.stack([off_cos, -off_sin], 1)
    part = dot("kip,prc->kirc", off, values)
    own_rows = device * block + jnp.arange(block, dtype=jnp.int32)
    tw_cos, tw_sin = phase_table(offsets, own_rows, length_two)
    tw_cos = tw_cos[:, :, None]
    tw_sin = tw_sin[:, :, None]
    part = jnp.stack([part[:, 0] * tw_cos + part[:, 1] * tw_sin, part[:, 1] * tw_cos - part[:, 0] * tw_sin], 1)
    part = lax.all_to_all(part.astype(bf16), "seq", split_axis=0, concat_axis=2, tiled=True)
    table = jnp.stack([jnp.stack([res_cos, res_sin], 0), jnp.stack([-res_sin, res_cos], 0)], 0)
    nxt = dot("oisr,girc->gosc", table, part)
    re, im = nxt[:, 0], nxt[:, 1]
    spec_real, spec_imag = spectrum[0], spectrum[1]
    filt = jnp.stack([re * spec_real - im * spec_imag, re * spec_imag + im * spec_real], 1)
    back = dot("oisr,gosc->girc", table, filt)
    own_offsets = 2 * device + jnp.arange(2, dtype=jnp.int32)
    un_cos, un_sin = phase_table(own_offsets, residues, length_two)
    un_cos = un_cos[:, :, None]
    un_sin = un_sin[:, :, None]
    back = jnp.stack([back[:, 0] * un_cos - back[:, 1] * un_sin, back[:, 1] * un_cos + back[:, 0] * un_sin], 1)
    back = lax.all_to_all(back.astype(bf16), "seq", split_axis=2, concat_axis=0, tiled=True)
    field = dot("kip,kirc->prc", off, back) / length_two
    field = lax.all_to_all(field.astype(bf16), "seq", split_axis=0, concat_axis=1, tiled=True)
    return field.reshape(tokens, width)


def per_device(gate_rows, key_rows, value_rows, spectrum, skip_bias):
    product = (key_rows.astype(f32) * value_rows.astype(f32)).astype(bf16)
    cols = lax.all_to_all(product, "ch", split_axis=1, concat_axis=0, tiled=True)
    field = convolve(cols, spectrum)
    field = lax.all_to_all(field, "ch", split_axis=0, concat_axis=1, tiled=True)
    gated = gate_rows.astype(f32) * (field.astype(f32) + skip_bias[None, :] * product.astype(f32))
    return gated.astype(bf16)


def solution(mesh):
    placed = (
        P(("seq", "ch"), None),
        P(("seq", "ch"), None),
        P(("seq", "ch"), None),
        P(None, "seq", None, "ch"),
        P(),
    )
    return jax.shard_map(
        per_device, mesh=mesh, in_specs=placed, out_specs=P(("seq", "ch"), None), check_vma=False
    )
```

```python
import math

import jax
import jax.numpy as jnp
import numpy as np
from jax import lax
from jax.experimental import pallas as pl
from jax.experimental.pallas import tpu as pltpu
from jax.sharding import PartitionSpec as P

f32, bf16 = jnp.float32, jnp.bfloat16
MESH = pl.DeviceIdType.MESH
NX, NZ, NC, NY = 4, 8, 2, 4
LANES = 128
CHUNKS = 2


def split(a):
    hi = a.astype(np.float32).astype(jnp.bfloat16)
    lo = (a - hi.astype(np.float64)).astype(np.float32).astype(jnp.bfloat16)
    return np.stack([hi, lo])


def tables():
    k2 = np.arange(512)
    turn = 2 * np.pi * (np.outer(k2, k2) % 512) / 512
    cs = np.stack([np.cos(turn), np.sin(turn)]).astype(np.float32).astype(jnp.bfloat16)
    kx, kc, b = np.meshgrid(np.arange(4), np.arange(2), np.arange(2), indexing="ij")
    base = (32 * kx + 2 * kc + b).reshape(16)
    pz, px, pc = np.meshgrid(np.arange(8), np.arange(4), np.arange(2), indexing="ij")
    p = (16 * px + 2 * pz + pc).reshape(64)
    mix, mix_t, twist = [], [], []
    for z in range(8):
        k1 = base + 4 * z
        turn = 2 * np.pi * (np.outer(k1, p) % 128) / 128
        w = np.stack([np.cos(turn), -np.sin(turn)], 1).reshape(32, 64)
        mix.append(split(w))
        mix_t.append(split(w.T))
        rows = []
        for x in range(4):
            r = (128 * np.arange(4)[:, None] + 32 * x + np.arange(32)[None, :]).reshape(128)
            turn = 2 * np.pi * (np.outer(k1, r) % 65536) / 65536
            rows.append(np.concatenate([np.cos(turn), np.sin(turn)]))
        twist.append(np.stack(rows))
    twist = np.stack(twist).astype(np.float32)
    k1 = np.arange(128)
    turn = 2 * np.pi * (np.outer(k1, np.arange(512)) % 65536) / 65536
    back = np.stack([np.cos(turn), np.sin(turn)]) / 65536
    back = back.reshape(2, 64, 2, 4, 128).transpose(1, 0, 2, 3, 4).reshape(64, 16, 128).astype(np.float32)
    return cs, np.stack(mix), np.stack(mix_t), twist, back


def dot(a, b):
    return jnp.dot(a, b, preferred_element_type=f32)


def kernel(
    gate_in, key_in, value_in, spec_in, cs_in, mix_in, mixt_in, twist_in, back_in, bias_ref, out_ref,
    gate_v, key_v, value_v, spec_v, cs_v, mix_s, mixt_s, twist_s, back_s,
    prod, gath, mixb, mixbt, tw, ti, ap, aa, ff, bb, cc, part, sbuf, rbuf, fs, fb,
    loc, s1s, s1r, ags, agr, s4s, s4r, s6s, s6r, rss, rsr, s9s, s9r,
):
    d = lax.axis_index("seq")
    y = lax.axis_index("ch")
    x, z, c = d // 16, (d // 2) % NZ, d % 2

    def seq_of(xx, zz, c_):
        return 16 * xx + 2 * zz + c_

    loads = [
        pltpu.make_async_copy(key_in, key_v, loc.at[0]),
        pltpu.make_async_copy(value_in, value_v, loc.at[1]),
        pltpu.make_async_copy(mix_in.at[z], mix_s, loc.at[2]),
        pltpu.make_async_copy(mixt_in.at[z], mixt_s, loc.at[3]),
        pltpu.make_async_copy(twist_in.at[z, x], twist_s, loc.at[4]),
        pltpu.make_async_copy(back_in.at[d], back_s, loc.at[5]),
        pltpu.make_async_copy(cs_in, cs_v, loc.at[6]),
        pltpu.make_async_copy(spec_in, spec_v, loc.at[7]),
        pltpu.make_async_copy(gate_in, gate_v, loc.at[8]),
    ]
    for load in loads:
        load.start()

    def peer(i):
        return (x + i // 8) % NX, (c + i // 4 % 2) % NC, (y + i % 4) % NY

    barrier = pltpu.get_barrier_semaphore()

    def greet(i, carry):
        xx, c_, yy = peer(i)
        pl.semaphore_signal(barrier, inc=1, device_id={"seq": seq_of(xx, z, c_), "ch": yy}, device_id_type=MESH)
        return carry

    lax.fori_loop(1, 32, greet, 0)
    up, down = seq_of(x, (z + 1) % NZ, c), seq_of(x, (z + NZ - 1) % NZ, c)
    for nb in (up, down):
        pl.semaphore_signal(barrier, inc=1, device_id={"seq": nb, "ch": y}, device_id_type=MESH)

    loads[0].wait()
    loads[1].wait()

    def block_columns(blk, q):
        return pl.ds(pl.multiple_of(512 * (blk // 8) + 256 * (blk // 4 % 2) + 128 * q, 128), LANES)

    for q in range(CHUNKS):
        for blk in range(32):
            rows, cols = pl.ds(32 * (blk % 4), 32), pl.ds(512 * (blk // 8) + 256 * (blk // 4 % 2) + 128 * q, LANES)
            prod[q, blk] = (key_v[rows, cols].astype(f32) * value_v[rows, cols].astype(f32)).astype(bf16)

    pl.semaphore_wait(barrier, 33)

    for q in range(CHUNKS):
        own = 8 * y + 4 * c + x
        pltpu.make_async_copy(prod.at[q, own], gath.at[q, z, 2 * x + c, y], s1r.at[q]).start()

        def spread(i, carry, q=q):
            xx, c_, yy = peer(i)
            pltpu.make_async_remote_copy(
                src_ref=prod.at[q, 8 * yy + 4 * c_ + xx],
                dst_ref=gath.at[q, z, 2 * x + c, y],
                send_sem=s1s.at[q],
                recv_sem=s1r.at[q],
                device_id={"seq": seq_of(xx, z, c_), "ch": yy},
                device_id_type=MESH,
            ).start()
            return carry

        lax.fori_loop(1, 32, spread, 0)

    for load in loads[2:6]:
        load.wait()
    big_r = lax.broadcasted_iota(jnp.int32, (512, 1024), 0) % 16
    big_c = lax.broadcasted_iota(jnp.int32, (512, 1024), 1) % 16
    e_r = (lax.broadcasted_iota(jnp.int32, (512, 32), 0) // 16 == lax.broadcasted_iota(jnp.int32, (512, 32), 1)).astype(f32).astype(bf16)
    e_c = (lax.broadcasted_iota(jnp.int32, (64, 1024), 1) // 16 == lax.broadcasted_iota(jnp.int32, (64, 1024), 0)).astype(f32).astype(bf16)
    for i in range(2):
        wide = dot(dot(e_r, mix_s[i]).astype(bf16), e_c)
        mixb[i] = jnp.where(big_r == big_c, wide, 0.0).astype(bf16)
    big_r = lax.broadcasted_iota(jnp.int32, (1024, 512), 0) % 16
    big_c = lax.broadcasted_iota(jnp.int32, (1024, 512), 1) % 16
    e_r = (lax.broadcasted_iota(jnp.int32, (1024, 64), 0) // 16 == lax.broadcasted_iota(jnp.int32, (1024, 64), 1)).astype(f32).astype(bf16)
    e_c = (lax.broadcasted_iota(jnp.int32, (32, 512), 1) // 16 == lax.broadcasted_iota(jnp.int32, (32, 512), 0)).astype(f32).astype(bf16)
    for i in range(2):
        wide = dot(dot(e_r, mixt_s[i]).astype(bf16), e_c)
        mixbt[i] = jnp.where(big_r == big_c, wide, 0.0).astype(bf16)

    def widen(k, carry):
        tw[k] = jnp.broadcast_to(twist_s[pl.ds(k, 1), :], (128, LANES)).T
        return carry

    lax.fori_loop(0, 32, widen, 0)

    def widen_back(k, carry):
        ti[k] = jnp.broadcast_to(back_s[pl.ds(k, 1), :], (128, LANES)).T
        return carry

    lax.fori_loop(0, 16, widen_back, 0)

    def wait_bytes(ref, sem):
        pltpu.make_async_copy(ref, ref, sem).wait()

    def ag_copy(q, way, s, h):
        slot = (z - (s - 1)) % NZ if way == 0 else (z + (s - 1)) % NZ
        ref = gath.at[q, slot, pl.ds(4 * h, 4)]
        return pltpu.make_async_remote_copy(
            src_ref=ref, dst_ref=ref, send_sem=ags.at[q], recv_sem=agr.at[q, way, s - 1, h],
            device_id={"seq": up if way == 0 else down, "ch": y}, device_id_type=MESH,
        )

    def ag_wait(q, way, s, h):
        slot = (z - s) % NZ if way == 0 else (z + s) % NZ
        wait_bytes(gath.at[q, slot, pl.ds(4 * h, 4)], agr.at[q, way, s - 1, h])

    def ag_begin(q):
        for h in range(2):
            for way in range(2):
                ag_copy(q, way, 1, h).start()

    def ag_step(q, s):
        for h in range(2):
            for way in range(2):
                ag_wait(q, way, s, h)
                if s < 3 or h == way:
                    ag_copy(q, way, s + 1, h).start()

    def ag_end(q):
        ag_wait(q, 0, 4, 0)
        ag_wait(q, 1, 4, 1)

    def mix(q):
        def body(v, carry):
            halves = [gath[q, :, :, v, pl.ds(16 * u, 16), :].reshape(1024, LANES) for u in range(2)]
            data = jnp.concatenate(halves, axis=1)
            got = (dot(mixb[0], data) + dot(mixb[1], data)).reshape(16, 2, 16, 2 * LANES)
            for u in range(2):
                re, im = got[:, 0, :, LANES * u : LANES * (u + 1)], got[:, 1, :, LANES * u : LANES * (u + 1)]
                rows = pl.ds(pl.multiple_of(32 * v + 16 * u, 16), 16)
                co, si = tw[pl.ds(0, 16), rows, :], tw[pl.ds(16, 16), rows, :]
                ap[q, :, 0, v, pl.ds(16 * u, 16), :] = (re * co + im * si).astype(bf16)
                ap[q, :, 1, v, pl.ds(16 * u, 16), :] = (im * co - re * si).astype(bf16)
            return carry

        lax.fori_loop(0, 4, body, 0)

    def s4_send(q):
        def to(i):
            return (x + i // 2) % NX, (c + i % 2) % NC

        own = ap.at[q, pl.ds(2 * (2 * x + c), 2)]
        pltpu.make_async_copy(own, aa.at[q, :, :, c, :, x], s4r.at[q]).start()
        for i in range(1, 8):
            xx, c_ = to(i)
            pltpu.make_async_remote_copy(
                src_ref=ap.at[q, pl.ds(2 * (2 * xx + c_), 2)], dst_ref=aa.at[q, :, :, c, :, x],
                send_sem=s4s.at[q], recv_sem=s4r.at[q],
                device_id={"seq": seq_of(xx, z, c_), "ch": y}, device_id_type=MESH,
            ).start()

    def lanes_of(ref, *at):
        return jnp.concatenate([ref[(*at, 0)], ref[(*at, 1)]], axis=-1)

    def filter_part(q, b):
        re = jnp.concatenate([aa[q, b, 0, i].reshape(512, LANES) for i in range(2)], axis=1)
        im = jnp.concatenate([aa[q, b, 1, i].reshape(512, LANES) for i in range(2)], axis=1)
        for t in range(2):
            rows = pl.ds(256 * t, 256)
            co, si = cs_v[0, rows, :], cs_v[1, rows, :]
            y_re = dot(co, re) + dot(si, im)
            y_im = dot(co, im) - dot(si, re)
            for i in range(2):
                cols = pl.ds(256 * i + 128 * q, LANES)
                h_re, h_im = spec_v[0, b, rows, cols], spec_v[1, b, rows, cols]
                part_re, part_im = y_re[:, LANES * i : LANES * (i + 1)], y_im[:, LANES * i : LANES * (i + 1)]
                ff[0, rows, pl.ds(LANES * i, LANES)] = (part_re * h_re - part_im * h_im).astype(bf16)
                ff[1, rows, pl.ds(LANES * i, LANES)] = (part_re * h_im + part_im * h_re).astype(bf16)
        re, im = ff[0], ff[1]
        for t in range(2):
            rows = pl.ds(256 * t, 256)
            co, si = cs_v[0, rows, :], cs_v[1, rows, :]
            g_re = dot(co, re) - dot(si, im)
            g_im = dot(co, im) + dot(si, re)
            for i in range(2):
                lanes = slice(LANES * i, LANES * (i + 1))
                for v in range(2):
                    t_co, t_si = ti[4 * b + 2 * t + v], ti[8 + 4 * b + 2 * t + v]
                    p_re, p_im = g_re[128 * v : 128 * (v + 1), lanes], g_im[128 * v : 128 * (v + 1), lanes]
                    bb[q, b, 0, i, 2 * t + v] = (p_re * t_co - p_im * t_si).astype(bf16).reshape(4, 32, LANES)
                    bb[q, b, 1, i, 2 * t + v] = (p_im * t_co + p_re * t_si).astype(bf16).reshape(4, 32, LANES)

    def s6_send(q):
        here = cc.at[q, pl.ds(2 * (2 * x + c), 2)]
        pltpu.make_async_copy(bb.at[q, :, :, c, :, x], here, s6r.at[q]).start()
        for i in range(1, 8):
            xx, c_ = (x + i // 2) % NX, (c + i % 2) % NC
            pltpu.make_async_remote_copy(
                src_ref=bb.at[q, :, :, c_, :, xx], dst_ref=here,
                send_sem=s6s.at[q], recv_sem=s6r.at[q],
                device_id={"seq": seq_of(xx, z, c_), "ch": y}, device_id_type=MESH,
            ).start()

    def unmix(q):
        def body(v, carry):
            halves = [cc[q, :, :, v, pl.ds(16 * u, 16), :].reshape(512, LANES) for u in range(2)]
            data = jnp.concatenate(halves, axis=1)
            got = (dot(mixbt[0], data) + dot(mixbt[1], data)).reshape(8, 8, 16, 2 * LANES)
            for u in range(2):
                part[q, :, :, v, pl.ds(16 * u, 16), :] = got[:, :, :, LANES * u : LANES * (u + 1)]
            return carry

        lax.fori_loop(0, 4, body, 0)

    def rs_step(q, s):
        for h in range(2):
            for way in range(2):
                if s == 1 and h != way:
                    continue
                target = (z + 5 - s) % NZ if way == 0 else (z + 3 + s) % NZ
                piece = pl.ds(4 * h, 4)
                has = s > 2 or (s == 2 and h == way)
                if has:
                    wait_bytes(rbuf.at[q, way, s - 2, piece], rsr.at[q, way, s - 2, h])
                for k in range(4):
                    total = part[q, target, 4 * h + k]
                    if has:
                        total = total + rbuf[q, way, s - 2, 4 * h + k].astype(f32)
                    sbuf[q, way, s - 1, 4 * h + k] = total.astype(bf16)
                pltpu.make_async_remote_copy(
                    src_ref=sbuf.at[q, way, s - 1, piece], dst_ref=rbuf.at[q, way, s - 1, piece],
                    send_sem=rss.at[q], recv_sem=rsr.at[q, way, s - 1, h],
                    device_id={"seq": up if way == 0 else down, "ch": y}, device_id_type=MESH,
                ).start()

    def rs_end(q):
        for h in range(2):
            for way in range(2):
                wait_bytes(rbuf.at[q, way, 3, pl.ds(4 * h, 4)], rsr.at[q, way, 3, h])
            for k in range(4 * h, 4 * h + 4):
                total = part[q, z, k] + (rbuf[q, 0, 3, k].astype(f32) + rbuf[q, 1, 3, k].astype(f32))
                fs[q, pl.ds(4 * k, 4)] = total.astype(bf16)
        own = 8 * y + 4 * c + x
        pltpu.make_async_copy(fs.at[q, 4 * (2 * x + c) + y], fb.at[q, own], s9r.at[q]).start()

        def give(i, carry):
            xx, c_, yy = peer(i)
            pltpu.make_async_remote_copy(
                src_ref=fs.at[q, 4 * (2 * xx + c_) + yy], dst_ref=fb.at[q, own],
                send_sem=s9s.at[q], recv_sem=s9r.at[q],
                device_id={"seq": seq_of(xx, z, c_), "ch": yy}, device_id_type=MESH,
            ).start()
            return carry

        lax.fori_loop(1, 32, give, 0)

    def finish(q):
        wait_bytes(fb.at[q], s9r.at[q])
        for blk in range(32):
            rows, cols = pl.ds(32 * (blk % 4), 32), pl.ds(512 * (blk // 8) + 256 * (blk // 4 % 2) + 128 * q, LANES)
            field = fb[q, blk].astype(f32) + bias_ref[:, cols] * prod[q, blk].astype(f32)
            out_ref[rows, cols] = (gate_v[rows, cols].astype(f32) * field).astype(bf16)

    wait_bytes(gath.at[0, z], s1r.at[0])
    ag_begin(0)
    wait_bytes(gath.at[1, z], s1r.at[1])
    ag_step(0, 1)
    ag_step(0, 2)
    ag_step(0, 3)
    ag_begin(1)
    ag_end(0)
    mix(0)
    s4_send(0)
    ag_step(1, 1)
    ag_step(1, 2)
    loads[6].wait()
    loads[7].wait()
    wait_bytes(aa.at[0], s4r.at[0])
    filter_part(0, 0)
    ag_step(1, 3)
    filter_part(0, 1)
    s6_send(0)
    ag_end(1)
    mix(1)
    s4_send(1)
    wait_bytes(cc.at[0], s6r.at[0])
    unmix(0)
    rs_step(0, 1)
    rs_step(0, 2)
    wait_bytes(aa.at[1], s4r.at[1])
    filter_part(1, 0)
    rs_step(0, 3)
    filter_part(1, 1)
    s6_send(1)
    rs_step(0, 4)
    wait_bytes(cc.at[1], s6r.at[1])
    unmix(1)
    rs_step(1, 1)
    rs_step(1, 2)
    rs_end(0)
    rs_step(1, 3)
    rs_step(1, 4)
    loads[8].wait()
    finish(0)
    rs_end(1)
    finish(1)

    for q in range(CHUNKS):
        wait_bytes(prod.at[q, pl.ds(0, 31)], s1s.at[q])
        wait_bytes(gath.at[q, pl.ds(0, 7)], ags.at[q])
        wait_bytes(ap.at[q, pl.ds(0, 14)], s4s.at[q])
        wait_bytes(cc.at[q, pl.ds(0, 14)], s6s.at[q])
        wait_bytes(gath.at[q, pl.ds(0, 7)], rss.at[q])
        wait_bytes(fs.at[q, pl.ds(0, 31)], s9s.at[q])


def per_device(gate_rows, key_rows, value_rows, spectrum, skip_bias):
    cs, mix, mix_t, twist, back = tables()
    anywhere = pl.BlockSpec(memory_space=pl.ANY)
    vmem = pl.BlockSpec(memory_space=pltpu.VMEM)
    rows, width = gate_rows.shape
    q = CHUNKS
    dma = pltpu.SemaphoreType.DMA
    return pl.pallas_call(
        kernel,
        out_shape=jax.ShapeDtypeStruct((rows, width), bf16),
        in_specs=[anywhere] * 9 + [vmem],
        out_specs=vmem,
        scratch_shapes=[
            pltpu.VMEM((rows, width), bf16),
            pltpu.VMEM((rows, width), bf16),
            pltpu.VMEM((rows, width), bf16),
            pltpu.VMEM((2, 2, 512, 512), f32),
            pltpu.VMEM((2, 512, 512), bf16),
            pltpu.VMEM((2, 32, 64), bf16),
            pltpu.VMEM((2, 64, 32), bf16),
            pltpu.VMEM((32, 128), f32),
            pltpu.VMEM((16, 128), f32),
            pltpu.VMEM((q, 32, 32, LANES), bf16),
            pltpu.VMEM((q, NZ, 8, 4, 32, LANES), bf16),
            pltpu.VMEM((2, 512, 1024), bf16),
            pltpu.VMEM((2, 1024, 512), bf16),
            pltpu.VMEM((32, 128, LANES), f32),
            pltpu.VMEM((16, 128, LANES), f32),
            pltpu.VMEM((q, 16, 2, 4, 32, LANES), bf16),
            pltpu.VMEM((q, 2, 2, 2, 4, 4, 32, LANES), bf16),
            pltpu.VMEM((2, 512, 2 * LANES), bf16),
            pltpu.VMEM((q, 2, 2, 2, 4, 4, 32, LANES), bf16),
            pltpu.VMEM((q, 16, 2, 4, 32, LANES), bf16),
            pltpu.VMEM((q, NZ, 8, 4, 32, LANES), f32),
            pltpu.VMEM((q, 2, 4, 8, 4, 32, LANES), bf16),
            pltpu.VMEM((q, 2, 4, 8, 4, 32, LANES), bf16),
            pltpu.VMEM((q, 32, 32, LANES), bf16),
            pltpu.VMEM((q, 32, 32, LANES), bf16),
            dma((9,)),
            dma((q,)), dma((q,)),
            dma((q,)), dma((q, 2, 4, 2)),
            dma((q,)), dma((q,)),
            dma((q,)), dma((q,)),
            dma((q,)), dma((q, 2, 4, 2)),
            dma((q,)), dma((q,)),
        ],
        compiler_params=pltpu.CompilerParams(
            collective_id=0, has_side_effects=True, vmem_limit_bytes=58 * 1024 * 1024
        ),
        name="hyena",
    )(gate_rows, key_rows, value_rows, spectrum, jnp.asarray(cs), jnp.asarray(mix), jnp.asarray(mix_t), jnp.asarray(twist), jnp.asarray(back), skip_bias.reshape(1, width))


def solution(mesh):
    placed = (
        P(("seq", "ch"), None),
        P(("seq", "ch"), None),
        P(("seq", "ch"), None),
        P(None, "seq", None, "ch"),
        P(),
    )
    return jax.shard_map(
        per_device, mesh=mesh, in_specs=placed, out_specs=P(("seq", "ch"), None), check_vma=False
    )
```

```python
import math

import jax
import jax.numpy as jnp
import numpy as np
from jax import lax
from jax.experimental import pallas as pl
from jax.experimental.pallas import tpu as pltpu
from jax.sharding import PartitionSpec as P

f32, bf16 = jnp.float32, jnp.bfloat16
MESH = pl.DeviceIdType.MESH
NX, NZ, NC, NY = 4, 8, 2, 4
LANES = 128
CHUNKS = 2


def split(a):
    hi = a.astype(np.float32).astype(jnp.bfloat16)
    lo = (a - hi.astype(np.float64)).astype(np.float32).astype(jnp.bfloat16)
    return np.stack([hi, lo])


def tables():
    k2 = np.arange(512)
    turn = 2 * np.pi * (np.outer(k2, k2) % 512) / 512
    cs = np.stack([np.cos(turn), np.sin(turn)]).astype(np.float32).astype(jnp.bfloat16)
    kx, kc, b = np.meshgrid(np.arange(4), np.arange(2), np.arange(2), indexing="ij")
    base = (32 * kx + 2 * kc + b).reshape(16)
    pz, px, pc = np.meshgrid(np.arange(8), np.arange(4), np.arange(2), indexing="ij")
    p = (16 * px + 2 * pz + pc).reshape(64)
    mix, mix_t, twist = [], [], []
    for z in range(8):
        k1 = base + 4 * z
        turn = 2 * np.pi * (np.outer(k1, p) % 128) / 128
        w = np.stack([np.cos(turn), -np.sin(turn)], 1).reshape(32, 64)
        mix.append(split(w))
        mix_t.append(split(w.T))
        rows = []
        for x in range(4):
            r = (128 * np.arange(4)[:, None] + 32 * x + np.arange(32)[None, :]).reshape(128)
            turn = 2 * np.pi * (np.outer(k1, r) % 65536) / 65536
            rows.append(np.concatenate([np.cos(turn), np.sin(turn)]))
        twist.append(np.stack(rows))
    twist = np.stack(twist).astype(np.float32)
    k1 = np.arange(128)
    turn = 2 * np.pi * (np.outer(k1, np.arange(512)) % 65536) / 65536
    back = np.stack([np.cos(turn), np.sin(turn)]) / 65536
    back = back.reshape(2, 64, 2, 4, 128).transpose(1, 0, 2, 3, 4).reshape(64, 16, 128).astype(np.float32)
    return cs, np.stack(mix), np.stack(mix_t), twist, back


def dot(a, b):
    return jnp.dot(a, b, preferred_element_type=f32)


def kernel(
    gate_in, key_in, value_in, spec_in, cs_in, mix_in, mixt_in, twist_in, back_in, bias_ref, out_ref,
    gate_v, key_v, value_v, spec_v, cs_v, mix_s, mixt_s, twist_s, back_s,
    prod, gath, mixb, mixbt, tw, ti, ap, aa, ff, bb, cc, part, sbuf, rbuf, fs, fb,
    loc, s1s, s1r, ags, agr, s4s, s4r, s6s, s6r, rss, rsr, s9s, s9r,
):
    d = lax.axis_index("seq")
    y = lax.axis_index("ch")
    x, z, c = d // 16, (d // 2) % NZ, d % 2

    def seq_of(xx, zz, c_):
        return 16 * xx + 2 * zz + c_

    loads = [
        pltpu.make_async_copy(key_in, key_v, loc.at[0]),
        pltpu.make_async_copy(value_in, value_v, loc.at[1]),
        pltpu.make_async_copy(mix_in.at[z], mix_s, loc.at[2]),
        pltpu.make_async_copy(mixt_in.at[z], mixt_s, loc.at[3]),
        pltpu.make_async_copy(twist_in.at[z, x], twist_s, loc.at[4]),
        pltpu.make_async_copy(back_in.at[d], back_s, loc.at[5]),
        pltpu.make_async_copy(cs_in, cs_v, loc.at[6]),
        pltpu.make_async_copy(spec_in, spec_v, loc.at[7]),
        pltpu.make_async_copy(gate_in, gate_v, loc.at[8]),
    ]
    loads[0].start()
    loads[1].start()

    def peer(i):
        return (x + i // 8) % NX, (c + i // 4 % 2) % NC, (y + i % 4) % NY

    barrier = pltpu.get_barrier_semaphore()

    def greet(i, carry):
        xx, c_, yy = peer(i)
        pl.semaphore_signal(barrier, inc=1, device_id={"seq": seq_of(xx, z, c_), "ch": yy}, device_id_type=MESH)
        return carry

    lax.fori_loop(1, 32, greet, 0)
    up, down = seq_of(x, (z + 1) % NZ, c), seq_of(x, (z + NZ - 1) % NZ, c)
    for nb in (up, down):
        pl.semaphore_signal(barrier, inc=1, device_id={"seq": nb, "ch": y}, device_id_type=MESH)

    def multiply(q):
        for blk in range(32):
            rows, cols = pl.ds(32 * (blk % 4), 32), pl.ds(512 * (blk // 8) + 256 * (blk // 4 % 2) + 128 * q, LANES)
            prod[q, blk] = (key_v[rows, cols].astype(f32) * value_v[rows, cols].astype(f32)).astype(bf16)

    def wait_bytes(ref, sem):
        pltpu.make_async_copy(ref, ref, sem).wait()

    own = 8 * y + 4 * c + x
    mine = 2 * x + c
    yh, yl = y // 2, y % 2

    def spread_all(q):
        there = gath.at[q, yh, z, mine, yl]
        pltpu.make_async_copy(prod.at[q, own], there, s1r.at[q, yh]).start()

        def spread(i, carry):
            xx, c_, yy = peer(i)
            pltpu.make_async_remote_copy(
                src_ref=prod.at[q, 8 * yy + 4 * c_ + xx],
                dst_ref=there,
                send_sem=s1s.at[q],
                recv_sem=s1r.at[q, yh],
                device_id={"seq": seq_of(xx, z, c_), "ch": yy},
                device_id_type=MESH,
            ).start()
            return carry

        lax.fori_loop(1, 32, spread, 0)

    def s1_wait(q, e):
        wait_bytes(gath.at[q, e, z], s1r.at[q, e])

    def one_hot(shape, axis):
        wide = lax.broadcasted_iota(jnp.int32, shape, axis) // 16
        return (wide == lax.broadcasted_iota(jnp.int32, shape, 1 - axis)).astype(f32).astype(bf16)

    def spread_table(small, big):
        rows, cols = small.shape[1], small.shape[2]
        diagonal = (lax.broadcasted_iota(jnp.int32, (16 * rows, 16 * cols), 0) % 16) == (
            lax.broadcasted_iota(jnp.int32, (16 * rows, 16 * cols), 1) % 16
        )
        for i in range(2):
            tall = dot(one_hot((16 * rows, rows), 0), small[i]).astype(bf16)
            wide = dot(tall, one_hot((cols, 16 * cols), 1))
            big[i] = jnp.where(diagonal, wide, 0.0).astype(bf16)

    def widen(k, carry):
        tw[k] = jnp.broadcast_to(twist_s[pl.ds(k, 1), :], (128, LANES)).T
        return carry

    def widen_back(k, carry):
        ti[k] = jnp.broadcast_to(back_s[pl.ds(k, 1), :], (128, LANES)).T
        return carry

    def ag_copy(q, e, way, s, h):
        slot = (z - (s - 1)) % NZ if way == 0 else (z + (s - 1)) % NZ
        ref = gath.at[q, e, slot, pl.ds(4 * h, 4)]
        return pltpu.make_async_remote_copy(
            src_ref=ref, dst_ref=ref, send_sem=ags.at[q, e], recv_sem=agr.at[q, e, way, s - 1, h],
            device_id={"seq": up if way == 0 else down, "ch": y}, device_id_type=MESH,
        )

    def ag_wait(q, e, way, s, h):
        slot = (z - s) % NZ if way == 0 else (z + s) % NZ
        wait_bytes(gath.at[q, e, slot, pl.ds(4 * h, 4)], agr.at[q, e, way, s - 1, h])

    def ag_begin(q, e):
        for h in range(2):
            for way in range(2):
                ag_copy(q, e, way, 1, h).start()

    def ag_step(q, e, s):
        for h in range(2):
            for way in range(2):
                ag_wait(q, e, way, s, h)
                if s < 3 or h == way:
                    ag_copy(q, e, way, s + 1, h).start()

    def ag_end(q, e):
        ag_wait(q, e, 0, 4, 0)
        ag_wait(q, e, 1, 4, 1)

    def mix(q, e):
        def body(v, carry):
            halves = [gath[q, e, :, :, v, pl.ds(16 * u, 16), :].reshape(1024, LANES) for u in range(2)]
            data = jnp.concatenate(halves, axis=1)
            got = (dot(mixb[0], data) + dot(mixb[1], data)).reshape(16, 2, 16, 2 * LANES)
            for u in range(2):
                re, im = got[:, 0, :, LANES * u : LANES * (u + 1)], got[:, 1, :, LANES * u : LANES * (u + 1)]
                rows = pl.ds(pl.multiple_of(64 * e + 32 * v + 16 * u, 16), 16)
                co, si = tw[pl.ds(0, 16), rows, :], tw[pl.ds(16, 16), rows, :]
                ap[q, e, :, 0, v, pl.ds(16 * u, 16), :] = (re * co + im * si).astype(bf16)
                ap[q, e, :, 1, v, pl.ds(16 * u, 16), :] = (im * co - re * si).astype(bf16)
            return carry

        lax.fori_loop(0, 2, body, 0)

    def s4_send(q, e):
        there = aa.at[q, :, :, c, pl.ds(2 * e, 2), x]
        pltpu.make_async_copy(ap.at[q, e, pl.ds(2 * mine, 2)], there, s4r.at[q, e]).start()
        for i in range(1, 8):
            xx, c_ = (x + i // 2) % NX, (c + i % 2) % NC
            pltpu.make_async_remote_copy(
                src_ref=ap.at[q, e, pl.ds(2 * (2 * xx + c_), 2)], dst_ref=there,
                send_sem=s4s.at[q, e], recv_sem=s4r.at[q, e],
                device_id={"seq": seq_of(xx, z, c_), "ch": y}, device_id_type=MESH,
            ).start()

    def s4_wait(q):
        for e in range(2):
            wait_bytes(cc.at[q, e], s4r.at[q, e])

    def forward(q):
        for b in range(2):
            re = jnp.concatenate([aa[q, b, 0, i].reshape(512, LANES) for i in range(2)], axis=1)
            im = jnp.concatenate([aa[q, b, 1, i].reshape(512, LANES) for i in range(2)], axis=1)
            for t in range(2):
                rows = pl.ds(256 * t, 256)
                co, si = cs_v[0, rows, :], cs_v[1, rows, :]
                y_re = dot(co, re) + dot(si, im)
                y_im = dot(co, im) - dot(si, re)
                for i in range(2):
                    cols = pl.ds(256 * i + 128 * q, LANES)
                    h_re, h_im = spec_v[0, b, rows, cols], spec_v[1, b, rows, cols]
                    p_re, p_im = y_re[:, LANES * i : LANES * (i + 1)], y_im[:, LANES * i : LANES * (i + 1)]
                    ff[b, 0, rows, pl.ds(LANES * i, LANES)] = (p_re * h_re - p_im * h_im).astype(bf16)
                    ff[b, 1, rows, pl.ds(LANES * i, LANES)] = (p_re * h_im + p_im * h_re).astype(bf16)

    def inverse(q, e):
        rows = pl.ds(256 * e, 256)
        co, si = cs_v[0, rows, :], cs_v[1, rows, :]
        for b in range(2):
            re, im = ff[b, 0], ff[b, 1]
            g_re = dot(co, re) - dot(si, im)
            g_im = dot(co, im) + dot(si, re)
            for i in range(2):
                lanes = slice(LANES * i, LANES * (i + 1))
                for v in range(2):
                    t_co, t_si = ti[4 * b + 2 * e + v], ti[8 + 4 * b + 2 * e + v]
                    p_re, p_im = g_re[128 * v : 128 * (v + 1), lanes], g_im[128 * v : 128 * (v + 1), lanes]
                    bb[q, b, 0, i, 2 * e + v] = (p_re * t_co - p_im * t_si).astype(bf16).reshape(4, 32, LANES)
                    bb[q, b, 1, i, 2 * e + v] = (p_im * t_co + p_re * t_si).astype(bf16).reshape(4, 32, LANES)

    def s6_send(q, e):
        here = cc.at[q, e, pl.ds(2 * mine, 2)]
        pltpu.make_async_copy(bb.at[q, :, :, c, pl.ds(2 * e, 2), x], here, s6r.at[q, e]).start()
        for i in range(1, 8):
            xx, c_ = (x + i // 2) % NX, (c + i % 2) % NC
            pltpu.make_async_remote_copy(
                src_ref=bb.at[q, :, :, c_, pl.ds(2 * e, 2), xx], dst_ref=here,
                send_sem=s6s.at[q, e], recv_sem=s6r.at[q, e],
                device_id={"seq": seq_of(xx, z, c_), "ch": y}, device_id_type=MESH,
            ).start()

    def s6_wait(q, e):
        wait_bytes(cc.at[q, e], s6r.at[q, e])

    def unmix(q, e):
        def body(v, carry):
            halves = [cc[q, e, :, :, v, pl.ds(16 * u, 16), :].reshape(512, LANES) for u in range(2)]
            data = jnp.concatenate(halves, axis=1)
            got = (dot(mixbt[0], data) + dot(mixbt[1], data)).reshape(8, 8, 16, 2 * LANES)
            for u in range(2):
                part[q, e, :, :, v, pl.ds(16 * u, 16), :] = got[:, :, :, LANES * u : LANES * (u + 1)]
            return carry

        lax.fori_loop(0, 2, body, 0)

    def rs_step(q, e, s):
        for h in range(2):
            for way in range(2):
                if s == 1 and h != way:
                    continue
                target = (z + 5 - s) % NZ if way == 0 else (z + 3 + s) % NZ
                piece = pl.ds(4 * h, 4)
                has = s > 2 or (s == 2 and h == way)
                total = part[q, e, target, piece]
                if has:
                    wait_bytes(rbuf.at[q, e, way, s - 2, piece], rsr.at[q, e, way, s - 2, h])
                    total = total + rbuf[q, e, way, s - 2, piece].astype(f32)
                sbuf[q, e, way, s - 1, piece] = total.astype(bf16)
                pltpu.make_async_remote_copy(
                    src_ref=sbuf.at[q, e, way, s - 1, piece], dst_ref=rbuf.at[q, e, way, s - 1, piece],
                    send_sem=rss.at[q, e], recv_sem=rsr.at[q, e, way, s - 1, h],
                    device_id={"seq": up if way == 0 else down, "ch": y}, device_id_type=MESH,
                ).start()

    def rs_end(q, e):
        for h in range(2):
            piece = pl.ds(4 * h, 4)
            for way in range(2):
                wait_bytes(rbuf.at[q, e, way, 3, piece], rsr.at[q, e, way, 3, h])
            total = part[q, e, z, piece] + (rbuf[q, e, 0, 3, piece].astype(f32) + rbuf[q, e, 1, 3, piece].astype(f32))
            fs[q, e, pl.ds(8 * h, 8)] = total.astype(bf16).reshape(8, 32, LANES)

        def send(xx, c_, yy):
            pltpu.make_async_remote_copy(
                src_ref=fs.at[q, e, 2 * (2 * xx + c_) + yy - 2 * e], dst_ref=fb.at[q, own],
                send_sem=s9s.at[q], recv_sem=s9r.at[q],
                device_id={"seq": seq_of(xx, z, c_), "ch": yy}, device_id_type=MESH,
            ).start()

        def give(i, carry):
            send((x + i // 4) % NX, (c + i // 2 % 2) % NC, 2 * e + (y + i) % 2)
            return carry

        lax.fori_loop(2, 16, give, 0)
        for i in range(2):

            @pl.when(2 * e + i == y)
            def _():
                pltpu.make_async_copy(fs.at[q, e, 2 * mine + i], fb.at[q, own], s9r.at[q]).start()

            @pl.when(2 * e + i != y)
            def _():
                send(x, c, 2 * e + i)

    def finish(q):
        wait_bytes(fb.at[q], s9r.at[q])
        for blk in range(32):
            rows, cols = pl.ds(32 * (blk % 4), 32), pl.ds(512 * (blk // 8) + 256 * (blk // 4 % 2) + 128 * q, LANES)
            field = fb[q, blk].astype(f32) + bias_ref[:, cols] * prod[q, blk].astype(f32)
            out_ref[rows, cols] = (gate_v[rows, cols].astype(f32) * field).astype(bf16)

    loads[0].wait()
    loads[1].wait()
    multiply(0)
    pl.semaphore_wait(barrier, 33)
    spread_all(0)
    multiply(1)
    spread_all(1)
    for load in loads[2:]:
        load.start()
    s1_wait(0, 0)
    ag_begin(0, 0)
    s1_wait(0, 1)
    for load in loads[2:6]:
        load.wait()
    spread_table(mix_s, mixb)
    ag_step(0, 0, 1)
    lax.fori_loop(0, 32, widen, 0)
    ag_step(0, 0, 2)
    ag_begin(0, 1)
    ag_step(0, 0, 3)
    ag_end(0, 0)
    mix(0, 0)
    s4_send(0, 0)
    ag_step(0, 1, 1)
    lax.fori_loop(0, 16, widen_back, 0)
    ag_step(0, 1, 2)
    s1_wait(1, 0)
    ag_begin(1, 0)
    ag_step(0, 1, 3)
    ag_end(0, 1)
    mix(0, 1)
    s4_send(0, 1)
    ag_step(1, 0, 1)
    spread_table(mixt_s, mixbt)
    ag_step(1, 0, 2)
    s1_wait(1, 1)
    ag_begin(1, 1)
    for load in loads[6:]:
        load.wait()
    s4_wait(0)
    forward(0)
    ag_step(1, 0, 3)
    ag_end(1, 0)
    inverse(0, 0)
    s6_send(0, 0)
    ag_step(1, 1, 1)
    mix(1, 0)
    s4_send(1, 0)
    inverse(0, 1)
    s6_send(0, 1)
    ag_step(1, 1, 2)
    ag_step(1, 1, 3)
    s6_wait(0, 0)
    unmix(0, 0)
    rs_step(0, 0, 1)
    ag_end(1, 1)
    mix(1, 1)
    s4_send(1, 1)
    rs_step(0, 0, 2)
    s6_wait(0, 1)
    unmix(0, 1)
    rs_step(0, 0, 3)
    rs_step(0, 1, 1)
    rs_step(0, 0, 4)
    rs_step(0, 1, 2)
    s4_wait(1)
    forward(1)
    rs_end(0, 0)
    inverse(1, 0)
    s6_send(1, 0)
    rs_step(0, 1, 3)
    inverse(1, 1)
    s6_send(1, 1)
    rs_step(0, 1, 4)
    s6_wait(1, 0)
    unmix(1, 0)
    rs_step(1, 0, 1)
    rs_end(0, 1)
    rs_step(1, 0, 2)
    s6_wait(1, 1)
    unmix(1, 1)
    rs_step(1, 0, 3)
    rs_step(1, 1, 1)
    rs_step(1, 0, 4)
    rs_step(1, 1, 2)
    rs_end(1, 0)
    rs_step(1, 1, 3)
    finish(0)
    rs_step(1, 1, 4)
    rs_end(1, 1)
    finish(1)

    for q in range(CHUNKS):
        wait_bytes(prod.at[q, pl.ds(0, 31)], s1s.at[q])
        wait_bytes(prod.at[q, pl.ds(0, 31)], s9s.at[q])
        for e in range(2):
            wait_bytes(gath.at[q, e, pl.ds(0, 7)], ags.at[q, e])
            wait_bytes(ap.at[q, e, pl.ds(0, 14)], s4s.at[q, e])
            wait_bytes(cc.at[q, e, pl.ds(0, 14)], s6s.at[q, e])
            wait_bytes(gath.at[q, e, pl.ds(0, 7)], rss.at[q, e])


def per_device(gate_rows, key_rows, value_rows, spectrum, skip_bias):
    cs, mix, mix_t, twist, back = tables()
    anywhere = pl.BlockSpec(memory_space=pl.ANY)
    vmem = pl.BlockSpec(memory_space=pltpu.VMEM)
    rows, width = gate_rows.shape
    q = CHUNKS
    dma = pltpu.SemaphoreType.DMA
    return pl.pallas_call(
        kernel,
        out_shape=jax.ShapeDtypeStruct((rows, width), bf16),
        in_specs=[anywhere] * 9 + [vmem],
        out_specs=vmem,
        scratch_shapes=[
            pltpu.VMEM((rows, width), bf16),
            pltpu.VMEM((rows, width), bf16),
            pltpu.VMEM((rows, width), bf16),
            pltpu.VMEM((2, 2, 512, 512), f32),
            pltpu.VMEM((2, 512, 512), bf16),
            pltpu.VMEM((2, 32, 64), bf16),
            pltpu.VMEM((2, 64, 32), bf16),
            pltpu.VMEM((32, 128), f32),
            pltpu.VMEM((16, 128), f32),
            pltpu.VMEM((q, 32, 32, LANES), bf16),
            pltpu.VMEM((q, 2, NZ, 8, 2, 32, LANES), bf16),
            pltpu.VMEM((2, 512, 1024), bf16),
            pltpu.VMEM((2, 1024, 512), bf16),
            pltpu.VMEM((32, 128, LANES), f32),
            pltpu.VMEM((16, 128, LANES), f32),
            pltpu.VMEM((q, 2, 16, 2, 2, 32, LANES), bf16),
            pltpu.VMEM((q, 2, 2, 2, 4, 4, 32, LANES), bf16),
            pltpu.VMEM((2, 2, 512, 2 * LANES), bf16),
            pltpu.VMEM((q, 2, 2, 2, 4, 4, 32, LANES), bf16),
            pltpu.VMEM((q, 2, 16, 2, 2, 32, LANES), bf16),
            pltpu.VMEM((q, 2, NZ, 8, 2, 32, LANES), f32),
            pltpu.VMEM((q, 2, 2, 4, 8, 2, 32, LANES), bf16),
            pltpu.VMEM((q, 2, 2, 4, 8, 2, 32, LANES), bf16),
            pltpu.VMEM((q, 2, 16, 32, LANES), bf16),
            pltpu.VMEM((q, 32, 32, LANES), bf16),
            dma((9,)),
            dma((q,)), dma((q, 2)),
            dma((q, 2)), dma((q, 2, 2, 4, 2)),
            dma((q, 2)), dma((q, 2)),
            dma((q, 2)), dma((q, 2)),
            dma((q, 2)), dma((q, 2, 2, 4, 2)),
            dma((q,)), dma((q,)),
        ],
        compiler_params=pltpu.CompilerParams(
            collective_id=0, has_side_effects=True, vmem_limit_bytes=58 * 1024 * 1024
        ),
        name="hyena",
    )(gate_rows, key_rows, value_rows, spectrum, jnp.asarray(cs), jnp.asarray(mix), jnp.asarray(mix_t), jnp.asarray(twist), jnp.asarray(back), skip_bias.reshape(1, width))


def solution(mesh):
    placed = (
        P(("seq", "ch"), None),
        P(("seq", "ch"), None),
        P(("seq", "ch"), None),
        P(None, "seq", None, "ch"),
        P(),
    )
    return jax.shard_map(
        per_device, mesh=mesh, in_specs=placed, out_specs=P(("seq", "ch"), None), check_vma=False
    )
```

```python
import math

import jax
import jax.numpy as jnp
import numpy as np
from jax import lax
from jax.experimental import pallas as pl
from jax.experimental.pallas import tpu as pltpu
from jax.sharding import PartitionSpec as P

f32, bf16 = jnp.float32, jnp.bfloat16
MESH = pl.DeviceIdType.MESH
NX, NZ, NC, NY = 4, 8, 2, 4
LANES = 128
CHUNKS = 2


def split(a):
    hi = a.astype(np.float32).astype(jnp.bfloat16)
    lo = (a - hi.astype(np.float64)).astype(np.float32).astype(jnp.bfloat16)
    return np.stack([hi, lo])


def tables():
    k2 = np.arange(512)
    turn = 2 * np.pi * (np.outer(k2, k2) % 512) / 512
    cs = np.stack([np.cos(turn), np.sin(turn)]).astype(np.float32).astype(jnp.bfloat16)
    kx, kc, b = np.meshgrid(np.arange(4), np.arange(2), np.arange(2), indexing="ij")
    base = (32 * kx + 2 * kc + b).reshape(16)
    pz, px, pc = np.meshgrid(np.arange(8), np.arange(4), np.arange(2), indexing="ij")
    p = (16 * px + 2 * pz + pc).reshape(64)
    mix, mix_t, twist = [], [], []
    for z in range(8):
        k1 = base + 4 * z
        turn = 2 * np.pi * (np.outer(k1, p) % 128) / 128
        w = np.stack([np.cos(turn), -np.sin(turn)], 1).reshape(32, 64)
        mix.append(split(w))
        mix_t.append(split(w.T))
        rows = []
        for x in range(4):
            r = (128 * np.arange(4)[:, None] + 32 * x + np.arange(32)[None, :]).reshape(128)
            turn = 2 * np.pi * (np.outer(k1, r) % 65536) / 65536
            rows.append(np.concatenate([np.cos(turn), np.sin(turn)]))
        twist.append(np.stack(rows))
    twist = np.stack(twist).astype(np.float32)
    k1 = np.arange(128)
    turn = 2 * np.pi * (np.outer(k1, np.arange(512)) % 65536) / 65536
    back = np.stack([np.cos(turn), np.sin(turn)]) / 65536
    back = back.reshape(2, 64, 2, 4, 128).transpose(1, 0, 2, 3, 4).reshape(64, 16, 128).astype(np.float32)
    return cs, np.stack(mix), np.stack(mix_t), twist, back


def dot(a, b):
    return jnp.dot(a, b, preferred_element_type=f32)


def kernel(
    gate_in, key_in, value_in, spec_in, cs_in, mix_in, mixt_in, twist_in, back_in, bias_ref, out_ref,
    gate_v, key_v, value_v, spec_v, cs_v, mix_s, mixt_s, twist_s, back_s,
    prod, gath, mixb, mixbt, tw, ti, ap, aa, ff, bb, cc, part, sbuf, rbuf, fs, fb,
    loc, s1s, s1r, ags, agr, s4s, s4r, s6s, s6r, rss, rsr, s9s, s9r,
):
    d = lax.axis_index("seq")
    y = lax.axis_index("ch")
    x, z, c = d // 16, (d // 2) % NZ, d % 2

    def seq_of(xx, zz, c_):
        return 16 * xx + 2 * zz + c_

    loads = [
        pltpu.make_async_copy(key_in, key_v, loc.at[0]),
        pltpu.make_async_copy(value_in, value_v, loc.at[1]),
        pltpu.make_async_copy(mix_in.at[z], mix_s, loc.at[2]),
        pltpu.make_async_copy(mixt_in.at[z], mixt_s, loc.at[3]),
        pltpu.make_async_copy(twist_in.at[z, x], twist_s, loc.at[4]),
        pltpu.make_async_copy(back_in.at[d], back_s, loc.at[5]),
        pltpu.make_async_copy(cs_in, cs_v, loc.at[6]),
        pltpu.make_async_copy(spec_in, spec_v, loc.at[7]),
        pltpu.make_async_copy(gate_in, gate_v, loc.at[8]),
    ]
    loads[0].start()
    loads[1].start()

    def peer(i):
        return (x + i // 8) % NX, (c + i // 4 % 2) % NC, (y + i % 4) % NY

    barrier = pltpu.get_barrier_semaphore()

    def greet(i, carry):
        xx, c_, yy = peer(i)
        pl.semaphore_signal(barrier, inc=1, device_id={"seq": seq_of(xx, z, c_), "ch": yy}, device_id_type=MESH)
        return carry

    lax.fori_loop(1, 32, greet, 0)
    up, down = seq_of(x, (z + 1) % NZ, c), seq_of(x, (z + NZ - 1) % NZ, c)
    for nb in (up, down):
        pl.semaphore_signal(barrier, inc=1, device_id={"seq": nb, "ch": y}, device_id_type=MESH)

    def multiply(q):
        for blk in range(32):
            rows, cols = pl.ds(32 * (blk % 4), 32), pl.ds(512 * (blk // 8) + 256 * (blk // 4 % 2) + 128 * q, LANES)
            prod[q, blk] = (key_v[rows, cols].astype(f32) * value_v[rows, cols].astype(f32)).astype(bf16)

    def wait_bytes(ref, sem):
        pltpu.make_async_copy(ref, ref, sem).wait()

    own = 8 * y + 4 * c + x
    mine = 2 * x + c
    yh, yl = y // 2, y % 2

    def spread_all(q):
        there = gath.at[q, yh, z, mine, yl]
        pltpu.make_async_copy(prod.at[q, own], there, s1r.at[q, yh]).start()

        def spread(i, carry):
            xx, c_, yy = peer(i)
            pltpu.make_async_remote_copy(
                src_ref=prod.at[q, 8 * yy + 4 * c_ + xx],
                dst_ref=there,
                send_sem=s1s.at[q],
                recv_sem=s1r.at[q, yh],
                device_id={"seq": seq_of(xx, z, c_), "ch": yy},
                device_id_type=MESH,
            ).start()
            return carry

        lax.fori_loop(1, 32, spread, 0)

    def s1_wait(q, e):
        wait_bytes(gath.at[q, e, z], s1r.at[q, e])

    def one_hot(shape, axis):
        wide = lax.broadcasted_iota(jnp.int32, shape, axis) // 16
        return (wide == lax.broadcasted_iota(jnp.int32, shape, 1 - axis)).astype(f32).astype(bf16)

    def spread_table(small, big):
        rows, cols = small.shape[1], small.shape[2]
        diagonal = (lax.broadcasted_iota(jnp.int32, (16 * rows, 16 * cols), 0) % 16) == (
            lax.broadcasted_iota(jnp.int32, (16 * rows, 16 * cols), 1) % 16
        )
        for i in range(2):
            tall = dot(one_hot((16 * rows, rows), 0), small[i]).astype(bf16)
            wide = dot(tall, one_hot((cols, 16 * cols), 1))
            big[i] = jnp.where(diagonal, wide, 0.0).astype(bf16)

    def widen(k, carry):
        tw[k] = jnp.broadcast_to(twist_s[pl.ds(k, 1), :], (128, LANES)).T
        return carry

    def widen_back(k, carry):
        ti[k] = jnp.broadcast_to(back_s[pl.ds(k, 1), :], (128, LANES)).T
        return carry

    def ag_copy(q, e, way, s, h):
        slot = (z - (s - 1)) % NZ if way == 0 else (z + (s - 1)) % NZ
        ref = gath.at[q, e, slot, pl.ds(4 * h, 4)]
        return pltpu.make_async_remote_copy(
            src_ref=ref, dst_ref=ref, send_sem=ags.at[q, e], recv_sem=agr.at[q, e, way, s - 1, h],
            device_id={"seq": up if way == 0 else down, "ch": y}, device_id_type=MESH,
        )

    def ag_wait(q, e, way, s, h):
        slot = (z - s) % NZ if way == 0 else (z + s) % NZ
        wait_bytes(gath.at[q, e, slot, pl.ds(4 * h, 4)], agr.at[q, e, way, s - 1, h])

    def ag_begin(q, e, h):
        for way in range(2):
            ag_copy(q, e, way, 1, h).start()

    def ag_step(q, e, s, h):
        for way in range(2):
            ag_wait(q, e, way, s, h)
            if s < 3 or h == way:
                ag_copy(q, e, way, s + 1, h).start()

    def ag_end(q, e):
        ag_wait(q, e, 0, 4, 0)
        ag_wait(q, e, 1, 4, 1)

    def mix(q, e):
        def body(v, carry):
            halves = [gath[q, e, :, :, v, pl.ds(16 * u, 16), :].reshape(1024, LANES) for u in range(2)]
            data = jnp.concatenate(halves, axis=1)
            got = (dot(mixb[0], data) + dot(mixb[1], data)).reshape(16, 2, 16, 2 * LANES)
            for u in range(2):
                re, im = got[:, 0, :, LANES * u : LANES * (u + 1)], got[:, 1, :, LANES * u : LANES * (u + 1)]
                rows = pl.ds(pl.multiple_of(64 * e + 32 * v + 16 * u, 16), 16)
                co, si = tw[pl.ds(0, 16), rows, :], tw[pl.ds(16, 16), rows, :]
                ap[q, e, :, 0, v, pl.ds(16 * u, 16), :] = (re * co + im * si).astype(bf16)
                ap[q, e, :, 1, v, pl.ds(16 * u, 16), :] = (im * co - re * si).astype(bf16)
            return carry

        lax.fori_loop(0, 2, body, 0)

    def s4_send(q, e):
        there = aa.at[q, :, :, c, pl.ds(2 * e, 2), x]
        pltpu.make_async_copy(ap.at[q, e, pl.ds(2 * mine, 2)], there, s4r.at[q, e]).start()
        for i in range(1, 8):
            xx, c_ = (x + i // 2) % NX, (c + i % 2) % NC
            pltpu.make_async_remote_copy(
                src_ref=ap.at[q, e, pl.ds(2 * (2 * xx + c_), 2)], dst_ref=there,
                send_sem=s4s.at[q, e], recv_sem=s4r.at[q, e],
                device_id={"seq": seq_of(xx, z, c_), "ch": y}, device_id_type=MESH,
            ).start()

    def s4_wait(q):
        for e in range(2):
            wait_bytes(cc.at[q, e], s4r.at[q, e])

    def forward(q):
        for b in range(2):
            re = jnp.concatenate([aa[q, b, 0, i].reshape(512, LANES) for i in range(2)], axis=1)
            im = jnp.concatenate([aa[q, b, 1, i].reshape(512, LANES) for i in range(2)], axis=1)
            for t in range(2):
                rows = pl.ds(256 * t, 256)
                co, si = cs_v[0, rows, :], cs_v[1, rows, :]
                y_re = dot(co, re) + dot(si, im)
                y_im = dot(co, im) - dot(si, re)
                for i in range(2):
                    cols = pl.ds(256 * i + 128 * q, LANES)
                    h_re, h_im = spec_v[0, b, rows, cols], spec_v[1, b, rows, cols]
                    p_re, p_im = y_re[:, LANES * i : LANES * (i + 1)], y_im[:, LANES * i : LANES * (i + 1)]
                    ff[b, 0, rows, pl.ds(LANES * i, LANES)] = (p_re * h_re - p_im * h_im).astype(bf16)
                    ff[b, 1, rows, pl.ds(LANES * i, LANES)] = (p_re * h_im + p_im * h_re).astype(bf16)

    def inverse(q, e):
        rows = pl.ds(256 * e, 256)
        co, si = cs_v[0, rows, :], cs_v[1, rows, :]
        for b in range(2):
            re, im = ff[b, 0], ff[b, 1]
            g_re = dot(co, re) - dot(si, im)
            g_im = dot(co, im) + dot(si, re)
            for i in range(2):
                lanes = slice(LANES * i, LANES * (i + 1))
                for v in range(2):
                    t_co, t_si = ti[4 * b + 2 * e + v], ti[8 + 4 * b + 2 * e + v]
                    p_re, p_im = g_re[128 * v : 128 * (v + 1), lanes], g_im[128 * v : 128 * (v + 1), lanes]
                    bb[q, b, 0, i, 2 * e + v] = (p_re * t_co - p_im * t_si).astype(bf16).reshape(4, 32, LANES)
                    bb[q, b, 1, i, 2 * e + v] = (p_im * t_co + p_re * t_si).astype(bf16).reshape(4, 32, LANES)

    def s6_send(q, e):
        here = cc.at[q, e, pl.ds(2 * mine, 2)]
        pltpu.make_async_copy(bb.at[q, :, :, c, pl.ds(2 * e, 2), x], here, s6r.at[q, e]).start()
        for i in range(1, 8):
            xx, c_ = (x + i // 2) % NX, (c + i % 2) % NC
            pltpu.make_async_remote_copy(
                src_ref=bb.at[q, :, :, c_, pl.ds(2 * e, 2), xx], dst_ref=here,
                send_sem=s6s.at[q, e], recv_sem=s6r.at[q, e],
                device_id={"seq": seq_of(xx, z, c_), "ch": y}, device_id_type=MESH,
            ).start()

    def s6_wait(q, e):
        wait_bytes(cc.at[q, e], s6r.at[q, e])

    def unmix(q, e):
        def body(v, carry):
            halves = [cc[q, e, :, :, v, pl.ds(16 * u, 16), :].reshape(512, LANES) for u in range(2)]
            data = jnp.concatenate(halves, axis=1)
            got = (dot(mixbt[0], data) + dot(mixbt[1], data)).reshape(8, 8, 16, 2 * LANES)
            for u in range(2):
                part[q, e, :, :, v, pl.ds(16 * u, 16), :] = got[:, :, :, LANES * u : LANES * (u + 1)]
            return carry

        lax.fori_loop(0, 2, body, 0)

    def rs_step(q, e, s, h):
        for way in range(2):
            if s == 1 and h != way:
                continue
            target = (z + 5 - s) % NZ if way == 0 else (z + 3 + s) % NZ
            piece = pl.ds(4 * h, 4)
            has = s > 2 or (s == 2 and h == way)
            total = part[q, e, target, piece]
            if has:
                wait_bytes(rbuf.at[q, e, way, s - 2, piece], rsr.at[q, e, way, s - 2, h])
                total = total + rbuf[q, e, way, s - 2, piece].astype(f32)
            sbuf[q, e, way, s - 1, piece] = total.astype(bf16)
            pltpu.make_async_remote_copy(
                src_ref=sbuf.at[q, e, way, s - 1, piece], dst_ref=rbuf.at[q, e, way, s - 1, piece],
                send_sem=rss.at[q, e], recv_sem=rsr.at[q, e, way, s - 1, h],
                device_id={"seq": up if way == 0 else down, "ch": y}, device_id_type=MESH,
            ).start()


    def rs_end(q, e):
        for h in range(2):
            piece = pl.ds(4 * h, 4)
            for way in range(2):
                wait_bytes(rbuf.at[q, e, way, 3, piece], rsr.at[q, e, way, 3, h])
            total = part[q, e, z, piece] + (rbuf[q, e, 0, 3, piece].astype(f32) + rbuf[q, e, 1, 3, piece].astype(f32))
            fs[q, e, pl.ds(8 * h, 8)] = total.astype(bf16).reshape(8, 32, LANES)

        def send(xx, c_, yy):
            pltpu.make_async_remote_copy(
                src_ref=fs.at[q, e, 2 * (2 * xx + c_) + yy - 2 * e], dst_ref=fb.at[q, own],
                send_sem=s9s.at[q], recv_sem=s9r.at[q],
                device_id={"seq": seq_of(xx, z, c_), "ch": yy}, device_id_type=MESH,
            ).start()

        def give(i, carry):
            send((x + i // 4) % NX, (c + i // 2 % 2) % NC, 2 * e + (y + i) % 2)
            return carry

        lax.fori_loop(2, 16, give, 0)
        for i in range(2):

            @pl.when(2 * e + i == y)
            def _():
                pltpu.make_async_copy(fs.at[q, e, 2 * mine + i], fb.at[q, own], s9r.at[q]).start()

            @pl.when(2 * e + i != y)
            def _():
                send(x, c, 2 * e + i)

    def finish(q):
        wait_bytes(fb.at[q], s9r.at[q])
        for blk in range(32):
            rows, cols = pl.ds(32 * (blk % 4), 32), pl.ds(512 * (blk // 8) + 256 * (blk // 4 % 2) + 128 * q, LANES)
            field = fb[q, blk].astype(f32) + bias_ref[:, cols] * prod[q, blk].astype(f32)
            out_ref[rows, cols] = (gate_v[rows, cols].astype(f32) * field).astype(bf16)

    loads[0].wait()
    loads[1].wait()
    multiply(0)
    pl.semaphore_wait(barrier, 33)
    spread_all(0)
    for load in loads[2:]:
        load.start()
    s1_wait(0, 0)
    ag_begin(0, 0, 0)
    ag_begin(0, 0, 1)
    multiply(1)
    spread_all(1)
    s1_wait(0, 1)
    ag_begin(0, 1, 0)
    ag_begin(0, 1, 1)
    loads[4].wait()
    lax.fori_loop(0, 32, widen, 0)
    ag_step(0, 0, 1, 0)
    ag_step(0, 0, 1, 1)
    loads[2].wait()
    spread_table(mix_s, mixb)
    ag_step(0, 1, 1, 0)
    loads[3].wait()
    spread_table(mixt_s, mixbt)
    ag_step(0, 1, 1, 1)
    ag_step(0, 0, 2, 0)
    loads[5].wait()
    lax.fori_loop(0, 16, widen_back, 0)
    ag_step(0, 0, 2, 1)
    ag_step(0, 1, 2, 0)
    ag_step(0, 1, 2, 1)
    ag_step(0, 0, 3, 0)
    ag_step(0, 0, 3, 1)
    s1_wait(1, 0)
    ag_begin(1, 0, 1)
    ag_step(0, 1, 3, 0)
    ag_step(0, 1, 3, 1)
    ag_begin(1, 0, 0)
    ag_end(0, 0)
    mix(0, 0)
    s4_send(0, 0)
    ag_step(1, 0, 1, 1)
    s1_wait(1, 1)
    ag_begin(1, 1, 1)
    ag_end(0, 1)
    mix(0, 1)
    s4_send(0, 1)
    ag_step(1, 0, 1, 0)
    ag_begin(1, 1, 0)
    ag_step(1, 0, 2, 1)
    ag_step(1, 1, 1, 1)
    ag_step(1, 0, 2, 0)
    ag_step(1, 1, 1, 0)
    ag_step(1, 0, 3, 1)
    ag_step(1, 1, 2, 1)
    for load in loads[6:8]:
        load.wait()
    s4_wait(0)
    forward(0)
    inverse(0, 0)
    s6_send(0, 0)
    inverse(0, 1)
    s6_send(0, 1)
    ag_step(1, 0, 3, 0)
    ag_step(1, 1, 2, 0)
    ag_step(1, 1, 3, 1)
    ag_end(1, 0)
    mix(1, 0)
    s4_send(1, 0)
    ag_step(1, 1, 3, 0)
    s6_wait(0, 0)
    unmix(0, 0)
    rs_step(0, 0, 1, 0)
    rs_step(0, 0, 1, 1)
    ag_end(1, 1)
    mix(1, 1)
    s4_send(1, 1)
    rs_step(0, 0, 2, 0)
    rs_step(0, 0, 2, 1)
    s6_wait(0, 1)
    unmix(0, 1)
    rs_step(0, 1, 1, 1)
    rs_step(0, 1, 1, 0)
    rs_step(0, 0, 3, 0)
    rs_step(0, 0, 3, 1)
    rs_step(0, 1, 2, 1)
    rs_step(0, 1, 2, 0)
    rs_step(0, 0, 4, 0)
    rs_step(0, 0, 4, 1)
    rs_step(0, 1, 3, 1)
    s4_wait(1)
    forward(1)
    inverse(1, 0)
    s6_send(1, 0)
    inverse(1, 1)
    s6_send(1, 1)
    rs_step(0, 1, 3, 0)
    rs_end(0, 0)
    rs_step(0, 1, 4, 1)
    rs_step(0, 1, 4, 0)
    s6_wait(1, 0)
    unmix(1, 0)
    rs_step(1, 0, 1, 1)
    rs_step(1, 0, 1, 0)
    rs_end(0, 1)
    rs_step(1, 0, 2, 1)
    rs_step(1, 0, 2, 0)
    s6_wait(1, 1)
    unmix(1, 1)
    rs_step(1, 1, 1, 1)
    rs_step(1, 1, 1, 0)
    rs_step(1, 0, 3, 1)
    loads[8].wait()
    finish(0)
    rs_step(1, 0, 3, 0)
    rs_step(1, 1, 2, 1)
    rs_step(1, 1, 2, 0)
    rs_step(1, 0, 4, 1)
    rs_step(1, 0, 4, 0)
    rs_step(1, 1, 3, 1)
    rs_step(1, 1, 3, 0)
    rs_end(1, 0)
    rs_step(1, 1, 4, 1)
    rs_step(1, 1, 4, 0)
    rs_end(1, 1)
    finish(1)

    for q in range(CHUNKS):
        wait_bytes(prod.at[q, pl.ds(0, 31)], s1s.at[q])
        wait_bytes(prod.at[q, pl.ds(0, 31)], s9s.at[q])
        for e in range(2):
            wait_bytes(gath.at[q, e, pl.ds(0, 7)], ags.at[q, e])
            wait_bytes(ap.at[q, e, pl.ds(0, 14)], s4s.at[q, e])
            wait_bytes(cc.at[q, e, pl.ds(0, 14)], s6s.at[q, e])
            wait_bytes(gath.at[q, e, pl.ds(0, 7)], rss.at[q, e])


def per_device(gate_rows, key_rows, value_rows, spectrum, skip_bias):
    cs, mix, mix_t, twist, back = tables()
    anywhere = pl.BlockSpec(memory_space=pl.ANY)
    vmem = pl.BlockSpec(memory_space=pltpu.VMEM)
    rows, width = gate_rows.shape
    q = CHUNKS
    dma = pltpu.SemaphoreType.DMA
    return pl.pallas_call(
        kernel,
        out_shape=jax.ShapeDtypeStruct((rows, width), bf16),
        in_specs=[anywhere] * 9 + [vmem],
        out_specs=vmem,
        scratch_shapes=[
            pltpu.VMEM((rows, width), bf16),
            pltpu.VMEM((rows, width), bf16),
            pltpu.VMEM((rows, width), bf16),
            pltpu.VMEM((2, 2, 512, 512), f32),
            pltpu.VMEM((2, 512, 512), bf16),
            pltpu.VMEM((2, 32, 64), bf16),
            pltpu.VMEM((2, 64, 32), bf16),
            pltpu.VMEM((32, 128), f32),
            pltpu.VMEM((16, 128), f32),
            pltpu.VMEM((q, 32, 32, LANES), bf16),
            pltpu.VMEM((q, 2, NZ, 8, 2, 32, LANES), bf16),
            pltpu.VMEM((2, 512, 1024), bf16),
            pltpu.VMEM((2, 1024, 512), bf16),
            pltpu.VMEM((32, 128, LANES), f32),
            pltpu.VMEM((16, 128, LANES), f32),
            pltpu.VMEM((q, 2, 16, 2, 2, 32, LANES), bf16),
            pltpu.VMEM((q, 2, 2, 2, 4, 4, 32, LANES), bf16),
            pltpu.VMEM((2, 2, 512, 2 * LANES), bf16),
            pltpu.VMEM((q, 2, 2, 2, 4, 4, 32, LANES), bf16),
            pltpu.VMEM((q, 2, 16, 2, 2, 32, LANES), bf16),
            pltpu.VMEM((q, 2, NZ, 8, 2, 32, LANES), f32),
            pltpu.VMEM((q, 2, 2, 4, 8, 2, 32, LANES), bf16),
            pltpu.VMEM((q, 2, 2, 4, 8, 2, 32, LANES), bf16),
            pltpu.VMEM((q, 2, 16, 32, LANES), bf16),
            pltpu.VMEM((q, 32, 32, LANES), bf16),
            dma((9,)),
            dma((q,)), dma((q, 2)),
            dma((q, 2)), dma((q, 2, 2, 4, 2)),
            dma((q, 2)), dma((q, 2)),
            dma((q, 2)), dma((q, 2)),
            dma((q, 2)), dma((q, 2, 2, 4, 2)),
            dma((q,)), dma((q,)),
        ],
        compiler_params=pltpu.CompilerParams(
            collective_id=0, has_side_effects=True, vmem_limit_bytes=58 * 1024 * 1024
        ),
        name="hyena",
    )(gate_rows, key_rows, value_rows, spectrum, jnp.asarray(cs), jnp.asarray(mix), jnp.asarray(mix_t), jnp.asarray(twist), jnp.asarray(back), skip_bias.reshape(1, width))


def solution(mesh):
    placed = (
        P(("seq", "ch"), None),
        P(("seq", "ch"), None),
        P(("seq", "ch"), None),
        P(None, "seq", None, "ch"),
        P(),
    )
    return jax.shard_map(
        per_device, mesh=mesh, in_specs=placed, out_specs=P(("seq", "ch"), None), check_vma=False
    )
```

```python
import math

import jax
import jax.numpy as jnp
import numpy as np
from jax import lax
from jax.experimental import pallas as pl
from jax.experimental.pallas import tpu as pltpu
from jax.sharding import PartitionSpec as P

f32, bf16 = jnp.float32, jnp.bfloat16
MESH = pl.DeviceIdType.MESH
NX, NZ, NC, NY = 4, 8, 2, 4
LANES = 128
PASSES = 1


def split(a):
    hi = a.astype(np.float32).astype(jnp.bfloat16)
    lo = (a - hi.astype(np.float64)).astype(np.float32).astype(jnp.bfloat16)
    return np.stack([hi, lo])


def tables():
    nn, jh, nl, yy, i = np.meshgrid(*(np.arange(k) for k in (2, 2, 2, 4, 16)), indexing="ij")
    r = (128 * yy + 64 * jh + 32 * nn + 16 * nl + i).reshape(512)
    turn = 2 * np.pi * (np.outer(r, r) % 512) / 512
    cs = np.stack([split(np.cos(turn))[:PASSES], split(np.sin(turn))[:PASSES]], 1)
    kx, kc, b = np.meshgrid(np.arange(4), np.arange(2), np.arange(2), indexing="ij")
    base = (32 * kx + 2 * kc + b).reshape(16)
    pz, px, pc = np.meshgrid(np.arange(8), np.arange(4), np.arange(2), indexing="ij")
    p = (16 * px + 2 * pz + pc).reshape(64)
    mix, mix_t, twist = [], [], []
    for z in range(8):
        k1 = base + 4 * z
        turn = 2 * np.pi * (np.outer(k1, p) % 128) / 128
        w = np.stack([np.cos(turn), -np.sin(turn)], 1).reshape(32, 64)
        mix.append(split(w))
        mix_t.append(split(w.T / 65536))
        both = []
        for r in (np.arange(128), 128 * (np.arange(128) % 4)):
            turn = 2 * np.pi * (np.outer(k1, r) % 65536) / 65536
            both.append(np.concatenate([np.cos(turn), np.sin(turn)]))
        twist.append(np.stack(both))
    return cs, np.stack(mix), np.stack(mix_t), np.stack(twist).astype(np.float32)


def dot(a, b):
    return jnp.dot(a, b, preferred_element_type=f32)


def swap(a, b):
    left = lax.broadcasted_iota(jnp.int32, a.shape, a.ndim - 1) < LANES // 2
    ra, rb = pltpu.roll(a, LANES // 2, a.ndim - 1), pltpu.roll(b, LANES // 2, a.ndim - 1)
    return jnp.where(left, a, rb), jnp.where(left, ra, b)


def kernel(
    gate_in, key_in, value_in, spec_in, cs_in, mix_in, mixt_in, twist_in, bias_ref, out_ref,
    gate_v, key_v, value_v, spec_v, cs_v, mix_s, mixt_s, twist_s,
    prod, gath, mixb, mixbt, tw, aa, yacc, ff, cc, part, sbuf, rbuf, hs, hh, fs, fb,
    loc, s1s, s1r, ags, agr, hss, hsr, rss, rsr, s9s, s9r,
):
    d = lax.axis_index("seq")
    y = lax.axis_index("ch")
    x, z, c = d // 16, (d // 2) % NZ, d % 2

    def seq_of(xx, zz, c_):
        return 16 * xx + 2 * zz + c_

    loads = [
        pltpu.make_async_copy(key_in, key_v, loc.at[0]),
        pltpu.make_async_copy(value_in, value_v, loc.at[1]),
        pltpu.make_async_copy(mix_in.at[z], mix_s, loc.at[2]),
        pltpu.make_async_copy(mixt_in.at[z], mixt_s, loc.at[3]),
        pltpu.make_async_copy(twist_in.at[z], twist_s, loc.at[4]),
        pltpu.make_async_copy(spec_in, spec_v, loc.at[5]),
        pltpu.make_async_copy(cs_in, cs_v, loc.at[6]),
        pltpu.make_async_copy(gate_in, gate_v, loc.at[7]),
    ]
    loads[0].start()
    loads[1].start()

    def peer(i):
        return (x + i // 8) % NX, (c + i // 4 % 2) % NC, (y + i % 4) % NY

    barrier = pltpu.get_barrier_semaphore()

    def greet(i, carry):
        xx, c_, yy = peer(i)
        pl.semaphore_signal(barrier, inc=1, device_id={"seq": seq_of(xx, z, c_), "ch": yy}, device_id_type=MESH)
        return carry

    lax.fori_loop(1, 32, greet, 0)
    up, down = seq_of(x, (z + 1) % NZ, c), seq_of(x, (z + NZ - 1) % NZ, c)
    for nb in (up, down):
        pl.semaphore_signal(barrier, inc=1, device_id={"seq": nb, "ch": y}, device_id_type=MESH)

    def wait_bytes(ref, sem):
        pltpu.make_async_copy(ref, ref, sem).wait()

    mine = 2 * x + c
    own = 8 * y + mine

    def product_of(rows, cols):
        return (key_v[rows, cols].astype(f32) * value_v[rows, cols].astype(f32)).astype(bf16).astype(f32)

    def multiply(g):
        for t in range(16):
            cols = pl.ds(128 * t, LANES)
            pair = swap(product_of(pl.ds(32 * g, 32), cols), product_of(pl.ds(64 + 32 * g, 32), cols))
            for i in range(2):
                prod[g, 2 * t + i] = pair[i].astype(bf16).reshape(2, 16, LANES)

    def spread_all(g):
        there = gath.at[pl.ds(2 * g, 2), z, mine, y]
        pltpu.make_async_copy(prod.at[g, own], there, s1r.at[g]).start()

        def spread(i, carry):
            xx, c_, yy = peer(i)
            pltpu.make_async_remote_copy(
                src_ref=prod.at[g, 8 * yy + 2 * xx + c_],
                dst_ref=there,
                send_sem=s1s.at[g],
                recv_sem=s1r.at[g],
                device_id={"seq": seq_of(xx, z, c_), "ch": yy},
                device_id_type=MESH,
            ).start()
            return carry

        lax.fori_loop(1, 32, spread, 0)

    def s1_wait(g):
        wait_bytes(gath.at[pl.ds(2 * g, 2), z], s1r.at[g])

    def one_hot(shape, axis):
        wide = lax.broadcasted_iota(jnp.int32, shape, axis) // 16
        return (wide == lax.broadcasted_iota(jnp.int32, shape, 1 - axis)).astype(f32).astype(bf16)

    def spread_table(small, big):
        rows, cols = small.shape[1], small.shape[2]
        diagonal = (lax.broadcasted_iota(jnp.int32, (16 * rows, 16 * cols), 0) % 16) == (
            lax.broadcasted_iota(jnp.int32, (16 * rows, 16 * cols), 1) % 16
        )
        for i in range(2):
            tall = dot(one_hot((16 * rows, rows), 0), small[i]).astype(bf16)
            wide = dot(tall, one_hot((cols, 16 * cols), 1))
            big[i] = jnp.where(diagonal, wide, 0.0).astype(bf16)

    def widen(k, carry):
        left = lax.broadcasted_iota(jnp.int32, (64, LANES), 1) < LANES // 2
        columns = [jnp.broadcast_to(twist_s[0, pl.ds(k + 16 * i, 1), :], (128, LANES)).T for i in range(2)]
        co, si = (jnp.where(left, a[:64], a[64:]) for a in columns)
        turns = [twist_s[1, pl.ds(k + 16 * i, 1), :] for i in range(2)]
        for v in range(4):
            t_co, t_si = (jnp.broadcast_to(a[:, v : v + 1], (64, LANES)) for a in turns)
            tw[k, v] = co * t_co - si * t_si
            tw[16 + k, v] = si * t_co + co * t_si
        return carry

    def repack(m, carry):
        row = pl.multiple_of(128 * (m % 4) + 64 * (m // 8 % 2) + 32 * (m // 16) + 16 * (m // 4 % 2), 16)
        to = pl.ds(pl.multiple_of(16 * m, 16), 16)
        for t in range(4):
            for i in range(2):
                at = pl.ds(row, 16), pl.ds(128 * t, LANES)
                pair = swap(spec_v[(i, 0, *at)], spec_v[(i, 1, *at)])
                for k in range(2):
                    hs[2 * t + k, i, to, :] = pair[k].astype(bf16)
        return carry

    def filter_send():
        pltpu.make_async_copy(hs.at[mine], hh.at[mine], hsr).start()
        for i in range(1, 8):
            xx, c_ = (x + i // 2) % NX, (c + i % 2) % NC
            pltpu.make_async_remote_copy(
                src_ref=hs.at[2 * xx + c_], dst_ref=hh.at[mine], send_sem=hss, recv_sem=hsr,
                device_id={"seq": seq_of(xx, z, c_), "ch": y}, device_id_type=MESH,
            ).start()

    def ag_copy(n, way, s, h):
        slot = (z - (s - 1)) % NZ if way == 0 else (z + (s - 1)) % NZ
        ref = gath.at[n, slot, pl.ds(4 * h, 4)]
        return pltpu.make_async_remote_copy(
            src_ref=ref, dst_ref=ref, send_sem=ags.at[n], recv_sem=agr.at[n, way, s - 1, h],
            device_id={"seq": up if way == 0 else down, "ch": y}, device_id_type=MESH,
        )

    def ag_wait(n, way, s, h):
        slot = (z - s) % NZ if way == 0 else (z + s) % NZ
        wait_bytes(gath.at[n, slot, pl.ds(4 * h, 4)], agr.at[n, way, s - 1, h])

    def ag_begin(n, h):
        for way in range(2):
            ag_copy(n, way, 1, h).start()

    def ag_step(n, s, h):
        for way in range(2):
            ag_wait(n, way, s, h)
            if s < 3 or h == way:
                ag_copy(n, way, s + 1, h).start()

    def ag_end(n):
        ag_wait(n, 0, 4, 0)
        ag_wait(n, 1, 4, 1)

    def mix(n):
        def body(v, carry):
            halves = [gath[n, :, :, 2 * v + u].reshape(1024, LANES) for u in range(2)]
            data = jnp.concatenate(halves, axis=1)
            got = (dot(mixb[0], data) + dot(mixb[1], data)).reshape(8, 2, 2, 16, 2 * LANES)
            for u in range(2):
                lanes = slice(LANES * u, LANES * (u + 1))
                pairs = []
                for b in range(2):
                    re, im = got[:, b, 0, :, lanes], got[:, b, 1, :, lanes]
                    at = 2 * v + u, pl.ds(16 * n, 16)
                    co = jnp.stack([tw[(2 * k + b, *at)] for k in range(8)])
                    si = jnp.stack([tw[(16 + 2 * k + b, *at)] for k in range(8)])
                    pairs.append((re * co + im * si, im * co - re * si))
                for i in range(2):
                    for jh, tile in enumerate(swap(pairs[0][i], pairs[1][i])):
                        aa[i, :, n // 2, jh, n % 2, 2 * v + u] = tile.astype(bf16)
            return carry

        lax.fori_loop(0, 2, body, 0)

    def forward(g, w):
        re, im = (
            jnp.concatenate([aa[i, 2 * w + k, g].reshape(256, LANES) for k in range(2)], axis=1) for i in range(2)
        )
        y_re, y_im = (yacc[i, w] if g else 0.0 for i in range(2))
        for k in range(PASSES):
            co, si = cs_v[k, 0, :, pl.ds(256 * g, 256)], cs_v[k, 1, :, pl.ds(256 * g, 256)]
            y_re = y_re + (dot(co, re) + dot(si, im))
            y_im = y_im + (dot(co, im) - dot(si, re))
        if g == 0:
            yacc[0, w] = y_re
            yacc[1, w] = y_im
            return
        h_re, h_im = (
            jnp.concatenate([hh[2 * w + k, i] for k in range(2)], axis=1).astype(f32) for i in range(2)
        )
        ff[0, w] = (y_re * h_re - y_im * h_im).astype(bf16)
        ff[1, w] = (y_re * h_im + y_im * h_re).astype(bf16)

    def inverse(n):
        base = 256 * (n // 2) + 64 * (n % 2)
        tabs = [
            [jnp.concatenate([cs_v[k, i, pl.ds(base + 128 * jh, 64), :] for jh in range(2)], axis=0) for i in range(2)]
            for k in range(PASSES)
        ]
        for w in range(4):
            re, im = ff[0, w], ff[1, w]
            g_re = g_im = 0.0
            for co, si in tabs:
                g_re = g_re + (dot(co, re) - dot(si, im))
                g_im = g_im + (dot(co, im) + dot(si, re))
            for k in range(2):
                lanes = slice(LANES * k, LANES * (k + 1))
                b_re = swap(g_re[:64, lanes], g_re[64:, lanes])
                b_im = swap(g_im[:64, lanes], g_im[64:, lanes])
                for b in range(2):
                    f = 4 * w + 2 * k + b
                    co = tw[f, :, pl.ds(16 * n, 16), :].reshape(64, LANES)
                    si = tw[16 + f, :, pl.ds(16 * n, 16), :].reshape(64, LANES)
                    cc[n, 2 * f] = (b_re[b] * co - b_im[b] * si).astype(bf16).reshape(4, 16, LANES)
                    cc[n, 2 * f + 1] = (b_im[b] * co + b_re[b] * si).astype(bf16).reshape(4, 16, LANES)

    def unmix(n):
        def body(v, carry):
            halves = [cc[n, :, 2 * v + u].reshape(512, LANES) for u in range(2)]
            data = jnp.concatenate(halves, axis=1)
            got = (dot(mixbt[0], data) + dot(mixbt[1], data)).reshape(8, 8, 16, 2 * LANES)
            for u in range(2):
                part[n, :, :, 2 * v + u] = got[:, :, :, LANES * u : LANES * (u + 1)]
            return carry

        lax.fori_loop(0, 2, body, 0)

    def rs_step(n, s, h):
        for way in range(2):
            if s == 1 and h != way:
                continue
            target = (z + 5 - s) % NZ if way == 0 else (z + 3 + s) % NZ
            piece = pl.ds(4 * h, 4)
            has = s > 2 or (s == 2 and h == way)
            total = part[n, target, piece]
            if has:
                wait_bytes(rbuf.at[n, way, s - 2, piece], rsr.at[n, way, s - 2, h])
                total = total + rbuf[n, way, s - 2, piece].astype(f32)
            sbuf[n, way, s - 1, piece] = total.astype(bf16)
            pltpu.make_async_remote_copy(
                src_ref=sbuf.at[n, way, s - 1, piece], dst_ref=rbuf.at[n, way, s - 1, piece],
                send_sem=rss.at[n], recv_sem=rsr.at[n, way, s - 1, h],
                device_id={"seq": up if way == 0 else down, "ch": y}, device_id_type=MESH,
            ).start()

    def rs_end(n):
        for h in range(2):
            piece = pl.ds(4 * h, 4)
            for way in range(2):
                wait_bytes(rbuf.at[n, way, 3, piece], rsr.at[n, way, 3, h])
            total = part[n, z, piece] + (rbuf[n, 0, 3, piece].astype(f32) + rbuf[n, 1, 3, piece].astype(f32))
            fs[n // 2, pl.ds(16 * h, 16), n % 2] = total.astype(bf16).reshape(16, 16, LANES)

    def give_all(g):
        pltpu.make_async_copy(fs.at[g, 4 * mine + y], fb.at[g, own], s9r.at[g]).start()

        def give(i, carry):
            xx, c_, yy = peer(i)
            pltpu.make_async_remote_copy(
                src_ref=fs.at[g, 4 * (2 * xx + c_) + yy], dst_ref=fb.at[g, own],
                send_sem=s9s.at[g], recv_sem=s9r.at[g],
                device_id={"seq": seq_of(xx, z, c_), "ch": yy}, device_id_type=MESH,
            ).start()
            return carry

        lax.fori_loop(1, 32, give, 0)

    def finish(g):
        wait_bytes(fb.at[g], s9r.at[g])
        for t in range(16):
            cols = pl.ds(128 * t, LANES)
            pair = swap(*(fb[g, 2 * t + i].reshape(32, LANES).astype(f32) for i in range(2)))
            for jh in range(2):
                rows = pl.ds(64 * jh + 32 * g, 32)
                field = pair[jh] + bias_ref[:, cols] * product_of(rows, cols)
                out_ref[rows, cols] = (gate_v[rows, cols].astype(f32) * field).astype(bf16)

    loads[0].wait()
    loads[1].wait()
    multiply(0)
    pl.semaphore_wait(barrier, 33)
    spread_all(0)
    for load in loads[2:]:
        load.start()
    s1_wait(0)
    ag_begin(1, 1)
    ag_begin(1, 0)
    ag_begin(0, 0)
    multiply(1)
    spread_all(1)
    ag_step(1, 1, 1)
    ag_begin(0, 1)
    loads[5].wait()
    lax.fori_loop(0, 8, repack, 0)
    ag_step(1, 1, 0)
    lax.fori_loop(16, 24, repack, 0)
    lax.fori_loop(8, 16, repack, 0)
    ag_step(0, 1, 0)
    lax.fori_loop(24, 32, repack, 0)
    filter_send()
    ag_step(1, 2, 1)
    loads[2].wait()
    spread_table(mix_s, mixb)
    ag_step(0, 1, 1)
    loads[4].wait()
    lax.fori_loop(0, 4, widen, 0)
    loads[3].wait()
    spread_table(mixt_s, mixbt)
    ag_step(1, 2, 0)
    ag_step(0, 2, 0)
    lax.fori_loop(4, 8, widen, 0)
    lax.fori_loop(12, 16, widen, 0)
    ag_step(1, 3, 1)
    lax.fori_loop(8, 12, widen, 0)
    s1_wait(1)
    ag_begin(3, 1)
    ag_step(0, 2, 1)
    ag_step(1, 3, 0)
    ag_step(0, 3, 0)
    ag_begin(3, 0)
    ag_step(3, 1, 1)
    ag_step(0, 3, 1)
    ag_end(1)
    mix(1)
    ag_begin(2, 1)
    ag_begin(2, 0)
    ag_step(3, 1, 0)
    ag_step(3, 2, 1)
    ag_end(0)
    mix(0)
    ag_step(2, 1, 1)
    loads[6].wait()
    forward(0, 1)
    forward(0, 0)
    ag_step(2, 1, 0)
    forward(0, 2)
    forward(0, 3)
    ag_step(3, 2, 0)
    ag_step(3, 3, 1)
    ag_step(2, 2, 1)
    ag_step(2, 2, 0)
    ag_step(3, 3, 0)
    ag_step(2, 3, 1)
    ag_step(2, 3, 0)
    ag_end(3)
    mix(3)
    ag_end(2)
    mix(2)
    wait_bytes(hh, hsr)
    forward(1, 0)
    forward(1, 2)
    forward(1, 1)
    forward(1, 3)
    inverse(0)
    unmix(0)
    rs_step(0, 1, 1)
    rs_step(0, 1, 0)
    inverse(1)
    inverse(2)
    rs_step(0, 2, 1)
    rs_step(0, 2, 0)
    unmix(2)
    rs_step(2, 1, 1)
    rs_step(2, 1, 0)
    rs_step(0, 3, 1)
    unmix(1)
    rs_step(0, 3, 0)
    rs_step(2, 2, 1)
    inverse(3)
    rs_step(2, 2, 0)
    unmix(3)
    rs_step(0, 4, 1)
    rs_step(0, 4, 0)
    rs_step(2, 3, 1)
    rs_step(2, 3, 0)
    rs_step(1, 1, 0)
    rs_step(1, 1, 1)
    rs_end(0)
    rs_step(3, 1, 1)
    rs_step(3, 1, 0)
    rs_step(2, 4, 1)
    rs_step(2, 4, 0)
    rs_step(1, 2, 0)
    rs_step(1, 2, 1)
    rs_step(3, 2, 1)
    rs_step(3, 2, 0)
    rs_end(2)
    rs_step(1, 3, 0)
    rs_step(1, 3, 1)
    rs_step(3, 3, 1)
    rs_step(3, 3, 0)
    rs_step(1, 4, 0)
    rs_step(1, 4, 1)
    rs_step(3, 4, 1)
    rs_step(3, 4, 0)
    rs_end(1)
    give_all(0)
    rs_end(3)
    give_all(1)
    loads[7].wait()
    finish(0)
    finish(1)

    for g in range(2):
        wait_bytes(prod.at[g, pl.ds(0, 31)], s1s.at[g])
        wait_bytes(prod.at[g, pl.ds(0, 31)], s9s.at[g])
    wait_bytes(hs.at[pl.ds(0, 7)], hss)
    for n in range(4):
        wait_bytes(gath.at[n, pl.ds(0, 7)], ags.at[n])
        wait_bytes(gath.at[n, pl.ds(0, 7)], rss.at[n])


def per_device(gate_rows, key_rows, value_rows, spectrum, skip_bias):
    cs, mix, mix_t, twist = tables()
    anywhere = pl.BlockSpec(memory_space=pl.ANY)
    vmem = pl.BlockSpec(memory_space=pltpu.VMEM)
    rows, width = gate_rows.shape
    dma = pltpu.SemaphoreType.DMA
    return pl.pallas_call(
        kernel,
        out_shape=jax.ShapeDtypeStruct((rows, width), bf16),
        in_specs=[anywhere] * 8 + [vmem],
        out_specs=vmem,
        scratch_shapes=[
            pltpu.VMEM((rows, width), bf16),
            pltpu.VMEM((rows, width), bf16),
            pltpu.VMEM((rows, width), bf16),
            pltpu.VMEM((2, 2, 512, 512), f32),
            pltpu.VMEM((PASSES, 2, 512, 512), bf16),
            pltpu.VMEM((2, 32, 64), bf16),
            pltpu.VMEM((2, 64, 32), bf16),
            pltpu.VMEM((2, 32, 128), f32),
            pltpu.VMEM((2, 32, 2, 16, LANES), bf16),
            pltpu.VMEM((4, NZ, 8, 4, 16, LANES), bf16),
            pltpu.VMEM((2, 512, 1024), bf16),
            pltpu.VMEM((2, 1024, 512), bf16),
            pltpu.VMEM((32, 4, 64, LANES), f32),
            pltpu.VMEM((2, 8, 2, 2, 2, 4, 16, LANES), bf16),
            pltpu.VMEM((2, 4, 512, 2 * LANES), f32),
            pltpu.VMEM((2, 4, 512, 2 * LANES), bf16),
            pltpu.VMEM((4, 32, 4, 16, LANES), bf16),
            pltpu.VMEM((4, NZ, 8, 4, 16, LANES), f32),
            pltpu.VMEM((4, 2, 4, 8, 4, 16, LANES), bf16),
            pltpu.VMEM((4, 2, 4, 8, 4, 16, LANES), bf16),
            pltpu.VMEM((8, 2, 512, LANES), bf16),
            pltpu.VMEM((8, 2, 512, LANES), bf16),
            pltpu.VMEM((2, 32, 2, 16, LANES), bf16),
            pltpu.VMEM((2, 32, 2, 16, LANES), bf16),
            dma((8,)),
            dma((2,)), dma((2,)),
            dma((4,)), dma((4, 2, 4, 2)),
            dma, dma,
            dma((4,)), dma((4, 2, 4, 2)),
            dma((2,)), dma((2,)),
        ],
        compiler_params=pltpu.CompilerParams(
            collective_id=0, has_side_effects=True, vmem_limit_bytes=60 * 1024 * 1024
        ),
        name="hyena",
    )(gate_rows, key_rows, value_rows, spectrum, *(jnp.asarray(t) for t in (cs, mix, mix_t, twist)), skip_bias.reshape(1, width))


def solution(mesh):
    placed = (
        P(("seq", "ch"), None),
        P(("seq", "ch"), None),
        P(("seq", "ch"), None),
        P(None, "seq", None, "ch"),
        P(),
    )
    return jax.shard_map(
        per_device, mesh=mesh, in_specs=placed, out_specs=P(("seq", "ch"), None), check_vma=False
    )
```

```python
import math

import jax
import jax.numpy as jnp
import numpy as np
from jax import lax
from jax.experimental import pallas as pl
from jax.experimental.pallas import tpu as pltpu
from jax.sharding import PartitionSpec as P

f32, bf16 = jnp.float32, jnp.bfloat16
MESH = pl.DeviceIdType.MESH
NX, NZ, NC, NY = 4, 8, 2, 4
LANES = 128
PASSES = 1


def split(a):
    hi = a.astype(np.float32).astype(jnp.bfloat16)
    lo = (a - hi.astype(np.float64)).astype(np.float32).astype(jnp.bfloat16)
    return np.stack([hi, lo])


def tables():
    r = np.arange(512)
    turn = 2 * np.pi * (np.outer(r, r) % 512) / 512
    cs = np.stack([split(np.cos(turn))[:PASSES], split(np.sin(turn))[:PASSES]], 1)
    kx, kc, b = np.meshgrid(np.arange(4), np.arange(2), np.arange(2), indexing="ij")
    base = (32 * kx + 2 * kc + b).reshape(16)
    pz, px, pc = np.meshgrid(np.arange(8), np.arange(4), np.arange(2), indexing="ij")
    p = (16 * px + 2 * pz + pc).reshape(64)
    mix, mix_t, twist = [], [], []
    for z in range(8):
        k1 = base + 4 * z
        turn = 2 * np.pi * (np.outer(k1, p) % 128) / 128
        w = np.stack([np.cos(turn), -np.sin(turn)], 1).reshape(32, 64)
        mix.append(split(w))
        mix_t.append(split(w.T / 65536))
        both = []
        for r in (np.arange(128), 128 * (np.arange(128) % 4)):
            turn = 2 * np.pi * (np.outer(k1, r) % 65536) / 65536
            both.append(np.concatenate([np.cos(turn), np.sin(turn)]))
        twist.append(np.stack(both))
    return cs, np.stack(mix), np.stack(mix_t), np.stack(twist).astype(np.float32)


def dot(a, b):
    return jnp.dot(a, b, preferred_element_type=f32)


def swap(a, b):
    left = lax.broadcasted_iota(jnp.int32, a.shape, a.ndim - 1) < LANES // 2
    ra, rb = pltpu.roll(a, LANES // 2, a.ndim - 1), pltpu.roll(b, LANES // 2, a.ndim - 1)
    return jnp.where(left, a, rb), jnp.where(left, ra, b)


def kernel(
    gate_in, key_in, value_in, spec_in, cs_in, mix_in, mixt_in, twist_in, bias_ref, out_ref,
    gate_v, key_v, value_v, spec_v, cs_v, mix_s, mixt_s, twist_s,
    prod, gath, mixb, mixbt, tw, aa, yacc, ff, cc, part, sbuf, rbuf, hs, hh, fs, fb,
    loc, s1s, s1r, ags, agr, hss, hsr, rss, rsr, s9s, s9r,
):
    d = lax.axis_index("seq")
    y = lax.axis_index("ch")
    x, z, c = d // 16, (d // 2) % NZ, d % 2

    def seq_of(xx, zz, c_):
        return 16 * xx + 2 * zz + c_

    loads = [
        pltpu.make_async_copy(key_in, key_v, loc.at[0]),
        pltpu.make_async_copy(value_in, value_v, loc.at[1]),
        pltpu.make_async_copy(mix_in.at[z], mix_s, loc.at[2]),
        pltpu.make_async_copy(mixt_in.at[z], mixt_s, loc.at[3]),
        pltpu.make_async_copy(twist_in.at[z], twist_s, loc.at[4]),
        pltpu.make_async_copy(spec_in, spec_v, loc.at[5]),
        pltpu.make_async_copy(cs_in, cs_v, loc.at[6]),
        pltpu.make_async_copy(gate_in, gate_v, loc.at[7]),
    ]
    loads[0].start()
    loads[1].start()

    xs = [lax.rem(x + i, NX) for i in range(NX)]
    cores = [c, 1 - c]
    plane = [(2 * xx + c_, seq_of(xx, z, c_)) for xx in xs for c_ in cores]

    def each_peer(act):
        for place, seq in plane[1:]:
            act(place, seq, y)

        def others(i, carry):
            yy = lax.rem(y + i, NY)
            for place, seq in plane:
                act(place, seq, yy)
            return carry

        lax.fori_loop(1, NY, others, 0)

    barrier = pltpu.get_barrier_semaphore()

    def greet(place, seq, yy):
        pl.semaphore_signal(barrier, inc=1, device_id={"seq": seq, "ch": yy}, device_id_type=MESH)

    each_peer(greet)
    up, down = seq_of(x, (z + 1) % NZ, c), seq_of(x, (z + NZ - 1) % NZ, c)
    for nb in (up, down):
        pl.semaphore_signal(barrier, inc=1, device_id={"seq": nb, "ch": y}, device_id_type=MESH)

    def wait_bytes(ref, sem):
        pltpu.make_async_copy(ref, ref, sem).wait()

    mine = 2 * x + c
    own = 8 * y + mine

    after = [lax.rem(y + k, NY) for k in range(NY)]
    before = [lax.rem(y + NY - k, NY) for k in range(NY)]

    def columns_of(yy, t):
        return pl.ds(pl.multiple_of(512 * yy + 128 * t, 128), LANES)

    def product_of(rows, cols):
        return (key_v[rows, cols].astype(f32) * value_v[rows, cols].astype(f32)).astype(bf16).astype(f32)

    def multiply(k):
        for t in range(4):
            cols = columns_of(before[k], t)
            pair = swap(product_of(pl.ds(0, 64), cols), product_of(pl.ds(64, 64), cols))
            for i in range(2):
                prod[8 * before[k] + 2 * t + i] = pair[i].astype(bf16)

    def spread_all(k):
        there = gath.at[k, z, mine]
        if k == 0:
            pltpu.make_async_copy(prod.at[own], there, s1r.at[k]).start()
        for place, seq in plane[k == 0 :]:
            pltpu.make_async_remote_copy(
                src_ref=prod.at[8 * before[k] + place],
                dst_ref=there,
                send_sem=s1s,
                recv_sem=s1r.at[k],
                device_id={"seq": seq, "ch": before[k]},
                device_id_type=MESH,
            ).start()

    def s1_wait(k):
        wait_bytes(gath.at[k, z], s1r.at[k])

    def one_hot(shape, axis):
        wide = lax.broadcasted_iota(jnp.int32, shape, axis) // 16
        return (wide == lax.broadcasted_iota(jnp.int32, shape, 1 - axis)).astype(f32).astype(bf16)

    def spread_table(small, big):
        rows, cols = small.shape[1], small.shape[2]
        diagonal = (lax.broadcasted_iota(jnp.int32, (16 * rows, 16 * cols), 0) % 16) == (
            lax.broadcasted_iota(jnp.int32, (16 * rows, 16 * cols), 1) % 16
        )
        for i in range(2):
            tall = dot(one_hot((16 * rows, rows), 0), small[i]).astype(bf16)
            wide = dot(tall, one_hot((cols, 16 * cols), 1))
            big[i] = jnp.where(diagonal, wide, 0.0).astype(bf16)

    def widen(k, carry):
        left = lax.broadcasted_iota(jnp.int32, (64, LANES), 1) < LANES // 2
        columns = [jnp.broadcast_to(twist_s[0, pl.ds(k + 16 * i, 1), :], (128, LANES)).T for i in range(2)]
        co, si = (jnp.where(left, a[:64], a[64:]) for a in columns)
        turns = [twist_s[1, pl.ds(k + 16 * i, 1), :] for i in range(2)]
        for v in range(4):
            t_co, t_si = (jnp.broadcast_to(a[:, v : v + 1], (64, LANES)) for a in turns)
            tw[k, v] = co * t_co - si * t_si
            tw[16 + k, v] = si * t_co + co * t_si
        return carry

    def repack(m, carry):
        rows = pl.ds(pl.multiple_of(16 * m, 16), 16)
        for t in range(4):
            for i in range(2):
                at = rows, pl.ds(128 * t, LANES)
                pair = swap(spec_v[(i, 0, *at)], spec_v[(i, 1, *at)])
                for k in range(2):
                    hs[2 * t + k, i, rows, :] = pair[k].astype(bf16)
        return carry

    def filter_send():
        pltpu.make_async_copy(hs.at[mine], hh.at[mine], hsr).start()
        for place, seq in plane[1:]:
            pltpu.make_async_remote_copy(
                src_ref=hs.at[place], dst_ref=hh.at[mine], send_sem=hss, recv_sem=hsr,
                device_id={"seq": seq, "ch": y}, device_id_type=MESH,
            ).start()

    def ag_copy(n, way, s, h):
        slot = (z - (s - 1)) % NZ if way == 0 else (z + (s - 1)) % NZ
        ref = gath.at[n, slot, pl.ds(4 * h, 4)]
        return pltpu.make_async_remote_copy(
            src_ref=ref, dst_ref=ref, send_sem=ags.at[n], recv_sem=agr.at[n, way, s - 1, h],
            device_id={"seq": up if way == 0 else down, "ch": y}, device_id_type=MESH,
        )

    def ag_wait(n, way, s, h):
        slot = (z - s) % NZ if way == 0 else (z + s) % NZ
        wait_bytes(gath.at[n, slot, pl.ds(4 * h, 4)], agr.at[n, way, s - 1, h])

    def ag_begin(n, h):
        for way in range(2):
            ag_copy(n, way, 1, h).start()

    def ag_step(n, s, h):
        for way in range(2):
            ag_wait(n, way, s, h)
            if s < 3 or h == way:
                ag_copy(n, way, s + 1, h).start()

    def ag_end(n):
        ag_wait(n, 0, 4, 0)
        ag_wait(n, 1, 4, 1)

    def mix(n):
        def body(v, carry):
            rows = [pl.ds(pl.multiple_of(32 * v + 16 * u, 16), 16) for u in range(2)]
            halves = [gath[n, :, :, rows[u], :].reshape(1024, LANES) for u in range(2)]
            data = jnp.concatenate(halves, axis=1)
            got = (dot(mixb[0], data) + dot(mixb[1], data)).reshape(8, 2, 2, 16, 2 * LANES)
            for u in range(2):
                lanes = slice(LANES * u, LANES * (u + 1))
                pairs = []
                for b in range(2):
                    re, im = got[:, b, 0, :, lanes], got[:, b, 1, :, lanes]
                    at = after[n], rows[u]
                    co = jnp.stack([tw[(2 * k + b, *at)] for k in range(8)])
                    si = jnp.stack([tw[(16 + 2 * k + b, *at)] for k in range(8)])
                    pairs.append((re * co + im * si, im * co - re * si))
                for i in range(2):
                    for jh, tile in enumerate(swap(pairs[0][i], pairs[1][i])):
                        aa[i, :, after[n], jh, rows[u], :] = tile.astype(bf16)
            return carry

        lax.fori_loop(0, 2, body, 0)

    def forward(g, w):
        both = after[2 * g : 2 * g + 2]
        re, im = (
            jnp.concatenate(
                [jnp.concatenate([aa[i, 2 * w + k, yy].reshape(128, LANES) for k in range(2)], axis=1) for yy in both], axis=0
            )
            for i in range(2)
        )
        y_re, y_im = (yacc[i, w] if g else 0.0 for i in range(2))
        for k in range(PASSES):
            co, si = (
                jnp.concatenate([cs_v[k, i, :, pl.ds(pl.multiple_of(128 * yy, 128), 128)] for yy in both], axis=1)
                for i in range(2)
            )
            y_re = y_re + (dot(co, re) + dot(si, im))
            y_im = y_im + (dot(co, im) - dot(si, re))
        if g == 0:
            yacc[0, w] = y_re
            yacc[1, w] = y_im
            return
        h_re, h_im = (
            jnp.concatenate([hh[2 * w + k, i] for k in range(2)], axis=1).astype(f32) for i in range(2)
        )
        ff[0, w] = (y_re * h_re - y_im * h_im).astype(bf16)
        ff[1, w] = (y_re * h_im + y_im * h_re).astype(bf16)

    def inverse(n):
        rows = pl.ds(pl.multiple_of(128 * after[n], 128), 128)
        tabs = [[cs_v[k, i, rows, :] for i in range(2)] for k in range(PASSES)]
        for w in range(4):
            re, im = ff[0, w], ff[1, w]
            g_re = g_im = 0.0
            for co, si in tabs:
                g_re = g_re + (dot(co, re) - dot(si, im))
                g_im = g_im + (dot(co, im) + dot(si, re))
            for k in range(2):
                lanes = slice(LANES * k, LANES * (k + 1))
                b_re = swap(g_re[:64, lanes], g_re[64:, lanes])
                b_im = swap(g_im[:64, lanes], g_im[64:, lanes])
                for b in range(2):
                    f = 4 * w + 2 * k + b
                    co = tw[f, after[n]]
                    si = tw[16 + f, after[n]]
                    cc[n, 2 * f] = (b_re[b] * co - b_im[b] * si).astype(bf16)
                    cc[n, 2 * f + 1] = (b_im[b] * co + b_re[b] * si).astype(bf16)

    def unmix(n):
        def body(v, carry):
            rows = [pl.ds(pl.multiple_of(32 * v + 16 * u, 16), 16) for u in range(2)]
            halves = [cc[n, :, rows[u], :].reshape(512, LANES) for u in range(2)]
            data = jnp.concatenate(halves, axis=1)
            got = (dot(mixbt[0], data) + dot(mixbt[1], data)).reshape(8, 8, 16, 2 * LANES)
            for u in range(2):
                part[n, :, :, rows[u], :] = got[:, :, :, LANES * u : LANES * (u + 1)]
            return carry

        lax.fori_loop(0, 2, body, 0)

    def rs_step(n, s, h):
        for way in range(2):
            if s == 1 and h != way:
                continue
            target = (z + 5 - s) % NZ if way == 0 else (z + 3 + s) % NZ
            piece = pl.ds(4 * h, 4)
            has = s > 2 or (s == 2 and h == way)
            total = part[n, target, piece]
            if has:
                wait_bytes(rbuf.at[n, way, s - 2, piece], rsr.at[n, way, s - 2, h])
                total = total + rbuf[n, way, s - 2, piece].astype(f32)
            sbuf[n, way, s - 1, piece] = total.astype(bf16)
            pltpu.make_async_remote_copy(
                src_ref=sbuf.at[n, way, s - 1, piece], dst_ref=rbuf.at[n, way, s - 1, piece],
                send_sem=rss.at[n], recv_sem=rsr.at[n, way, s - 1, h],
                device_id={"seq": up if way == 0 else down, "ch": y}, device_id_type=MESH,
            ).start()

    def rs_end(n):
        for h in range(2):
            piece = pl.ds(4 * h, 4)
            for way in range(2):
                wait_bytes(rbuf.at[n, way, 3, piece], rsr.at[n, way, 3, h])
            total = part[n, z, piece] + (rbuf[n, 0, 3, piece].astype(f32) + rbuf[n, 1, 3, piece].astype(f32))
            fs[n, piece] = total.astype(bf16)

    def give_all(k):
        if k == 0:
            pltpu.make_async_copy(fs.at[k, mine], fb.at[own], s9r.at[k]).start()
        for place, seq in plane[k == 0 :]:
            pltpu.make_async_remote_copy(
                src_ref=fs.at[k, place], dst_ref=fb.at[own], send_sem=s9s, recv_sem=s9r.at[k],
                device_id={"seq": seq, "ch": after[k]}, device_id_type=MESH,
            ).start()

    def finish(k):
        wait_bytes(fb.at[pl.ds(8 * before[k], 8)], s9r.at[k])
        for t in range(4):
            cols = columns_of(before[k], t)
            pair = swap(*(fb[8 * before[k] + 2 * t + i].astype(f32) for i in range(2)))
            for jh in range(2):
                rows = pl.ds(64 * jh, 64)
                field = pair[jh] + bias_ref[:, cols] * product_of(rows, cols)
                out_ref[rows, cols] = (gate_v[rows, cols].astype(f32) * field).astype(bf16)

    loads[0].wait()
    loads[1].wait()
    multiply(0)
    pl.semaphore_wait(barrier, 33)
    spread_all(0)
    for load in loads[2:]:
        load.start()
    s1_wait(0)
    ag_begin(0, 0)
    ag_begin(0, 1)
    multiply(1)
    spread_all(1)
    loads[5].wait()
    lax.fori_loop(0, 8, repack, 0)
    loads[4].wait()
    lax.fori_loop(0, 4, widen, 0)
    lax.fori_loop(8, 16, repack, 0)
    ag_step(0, 1, 0)
    multiply(2)
    spread_all(2)
    ag_step(0, 1, 1)
    lax.fori_loop(16, 24, repack, 0)
    s1_wait(1)
    ag_begin(1, 0)
    ag_begin(1, 1)
    lax.fori_loop(4, 8, widen, 0)
    ag_step(0, 2, 0)
    multiply(3)
    spread_all(3)
    lax.fori_loop(24, 32, repack, 0)
    ag_step(0, 2, 1)
    filter_send()
    lax.fori_loop(8, 12, widen, 0)
    ag_step(1, 1, 0)
    loads[2].wait()
    spread_table(mix_s, mixb)
    ag_step(1, 1, 1)
    lax.fori_loop(12, 16, widen, 0)
    ag_step(0, 3, 0)
    loads[3].wait()
    spread_table(mixt_s, mixbt)
    ag_step(0, 3, 1)
    s1_wait(2)
    ag_begin(2, 0)
    ag_step(1, 2, 0)
    ag_step(1, 2, 1)
    ag_end(0)
    mix(0)
    ag_step(2, 1, 0)
    ag_begin(2, 1)
    ag_step(1, 3, 0)
    s1_wait(3)
    ag_begin(3, 0)
    ag_step(1, 3, 1)
    ag_step(2, 2, 0)
    ag_step(2, 1, 1)
    ag_begin(3, 1)
    ag_step(3, 1, 0)
    ag_end(1)
    mix(1)
    ag_step(2, 3, 0)
    loads[6].wait()
    forward(0, 2)
    forward(0, 0)
    forward(0, 1)
    ag_step(2, 2, 1)
    forward(0, 3)
    ag_step(3, 1, 1)
    ag_step(3, 2, 0)
    ag_step(2, 3, 1)
    ag_step(3, 2, 1)
    ag_step(3, 3, 0)
    ag_end(2)
    mix(2)
    ag_step(3, 3, 1)
    ag_end(3)
    mix(3)
    wait_bytes(hh, hsr)
    forward(1, 1)
    forward(1, 3)
    forward(1, 0)
    forward(1, 2)
    inverse(0)
    unmix(0)
    rs_step(0, 1, 0)
    rs_step(0, 1, 1)
    inverse(1)
    inverse(2)
    rs_step(0, 2, 0)
    unmix(1)
    rs_step(0, 2, 1)
    rs_step(1, 1, 0)
    rs_step(1, 1, 1)
    rs_step(0, 3, 0)
    unmix(2)
    rs_step(0, 3, 1)
    inverse(3)
    rs_step(1, 2, 0)
    rs_step(1, 2, 1)
    unmix(3)
    rs_step(0, 4, 0)
    rs_step(0, 4, 1)
    rs_step(1, 3, 0)
    rs_step(1, 3, 1)
    rs_step(2, 1, 0)
    rs_step(2, 1, 1)
    rs_end(0)
    give_all(0)
    rs_step(3, 1, 0)
    rs_step(1, 4, 0)
    rs_step(3, 1, 1)
    rs_step(1, 4, 1)
    rs_step(2, 2, 0)
    rs_step(2, 2, 1)
    loads[7].wait()
    finish(0)
    rs_step(3, 2, 0)
    rs_step(3, 2, 1)
    rs_end(1)
    give_all(1)
    rs_step(2, 3, 0)
    rs_step(2, 3, 1)
    rs_step(3, 3, 0)
    finish(1)
    rs_step(3, 3, 1)
    rs_step(2, 4, 0)
    rs_step(2, 4, 1)
    rs_step(3, 4, 0)
    rs_step(3, 4, 1)
    rs_end(2)
    give_all(2)
    rs_end(3)
    give_all(3)
    finish(2)
    finish(3)

    wait_bytes(prod.at[pl.ds(0, 31)], s1s)
    wait_bytes(prod.at[pl.ds(0, 31)], s9s)
    wait_bytes(hs.at[pl.ds(0, 7)], hss)
    for n in range(4):
        wait_bytes(gath.at[n, pl.ds(0, 7)], ags.at[n])
        wait_bytes(gath.at[n, pl.ds(0, 7)], rss.at[n])


def per_device(gate_rows, key_rows, value_rows, spectrum, skip_bias):
    cs, mix, mix_t, twist = tables()
    anywhere = pl.BlockSpec(memory_space=pl.ANY)
    vmem = pl.BlockSpec(memory_space=pltpu.VMEM)
    rows, width = gate_rows.shape
    dma = pltpu.SemaphoreType.DMA
    return pl.pallas_call(
        kernel,
        out_shape=jax.ShapeDtypeStruct((rows, width), bf16),
        in_specs=[anywhere] * 8 + [vmem],
        out_specs=vmem,
        scratch_shapes=[
            pltpu.VMEM((rows, width), bf16),
            pltpu.VMEM((rows, width), bf16),
            pltpu.VMEM((rows, width), bf16),
            pltpu.VMEM((2, 2, 512, 512), f32),
            pltpu.VMEM((PASSES, 2, 512, 512), bf16),
            pltpu.VMEM((2, 32, 64), bf16),
            pltpu.VMEM((2, 64, 32), bf16),
            pltpu.VMEM((2, 32, 128), f32),
            pltpu.VMEM((32, 64, LANES), bf16),
            pltpu.VMEM((4, NZ, 8, 64, LANES), bf16),
            pltpu.VMEM((2, 512, 1024), bf16),
            pltpu.VMEM((2, 1024, 512), bf16),
            pltpu.VMEM((32, 4, 64, LANES), f32),
            pltpu.VMEM((2, 8, 4, 2, 64, LANES), bf16),
            pltpu.VMEM((2, 4, 512, 2 * LANES), f32),
            pltpu.VMEM((2, 4, 512, 2 * LANES), bf16),
            pltpu.VMEM((4, 32, 64, LANES), bf16),
            pltpu.VMEM((4, NZ, 8, 64, LANES), f32),
            pltpu.VMEM((4, 2, 4, 8, 64, LANES), bf16),
            pltpu.VMEM((4, 2, 4, 8, 64, LANES), bf16),
            pltpu.VMEM((8, 2, 512, LANES), bf16),
            pltpu.VMEM((8, 2, 512, LANES), bf16),
            pltpu.VMEM((4, 8, 64, LANES), bf16),
            pltpu.VMEM((32, 64, LANES), bf16),
            dma((8,)),
            dma, dma((4,)),
            dma((4,)), dma((4, 2, 4, 2)),
            dma, dma,
            dma((4,)), dma((4, 2, 4, 2)),
            dma, dma((4,)),
        ],
        compiler_params=pltpu.CompilerParams(
            collective_id=0, has_side_effects=True, vmem_limit_bytes=60 * 1024 * 1024
        ),
        name="hyena",
    )(gate_rows, key_rows, value_rows, spectrum, *(jnp.asarray(t) for t in (cs, mix, mix_t, twist)), skip_bias.reshape(1, width))


def solution(mesh):
    placed = (
        P(("seq", "ch"), None),
        P(("seq", "ch"), None),
        P(("seq", "ch"), None),
        P(None, "seq", None, "ch"),
        P(),
    )
    return jax.shard_map(
        per_device, mesh=mesh, in_specs=placed, out_specs=P(("seq", "ch"), None), check_vma=False
    )
```

```python
import math

import jax
import jax.numpy as jnp
import numpy as np
from jax import lax
from jax.experimental import pallas as pl
from jax.experimental.pallas import tpu as pltpu
from jax.sharding import PartitionSpec as P

f32, bf16 = jnp.float32, jnp.bfloat16
MESH = pl.DeviceIdType.MESH
NX, NZ, NC, NY = 4, 8, 2, 4
LANES = 128
PASSES = 1


def split(a):
    hi = a.astype(np.float32).astype(jnp.bfloat16)
    lo = (a - hi.astype(np.float64)).astype(np.float32).astype(jnp.bfloat16)
    return np.stack([hi, lo])


def tables():
    r = np.arange(512)
    turn = 2 * np.pi * (np.outer(r, r) % 512) / 512
    cs = np.stack([split(np.cos(turn))[:PASSES], split(np.sin(turn))[:PASSES]], 1)
    kx, kc, b = np.meshgrid(np.arange(4), np.arange(2), np.arange(2), indexing="ij")
    base = (32 * kx + 2 * kc + b).reshape(16)
    pz, px, pc = np.meshgrid(np.arange(8), np.arange(4), np.arange(2), indexing="ij")
    p = (16 * px + 2 * pz + pc).reshape(64)
    mix, mix_t, twist = [], [], []
    for z in range(8):
        k1 = base + 4 * z
        turn = 2 * np.pi * (np.outer(k1, p) % 128) / 128
        w = np.stack([np.cos(turn), -np.sin(turn)], 1).reshape(32, 64)
        mix.append(split(w))
        mix_t.append(split(w.T / 65536))
        both = []
        for r in (np.arange(128), 128 * (np.arange(128) % 4)):
            turn = 2 * np.pi * (np.outer(k1, r) % 65536) / 65536
            both.append(np.concatenate([np.cos(turn), np.sin(turn)]))
        twist.append(np.stack(both))
    return cs, np.stack(mix), np.stack(mix_t), np.stack(twist).astype(np.float32)


def dot(a, b):
    return jnp.dot(a, b, preferred_element_type=f32)


def swap(a, b):
    left = lax.broadcasted_iota(jnp.int32, a.shape, a.ndim - 1) < LANES // 2
    ra, rb = pltpu.roll(a, LANES // 2, a.ndim - 1), pltpu.roll(b, LANES // 2, a.ndim - 1)
    return jnp.where(left, a, rb), jnp.where(left, ra, b)


def kernel(
    gate_in, key_in, value_in, spec_in, cs_in, mix_in, mixt_in, twist_in, bias_ref, out_ref,
    gate_v, key_v, value_v, spec_v, cs_v, mix_s, mixt_s, twist_s,
    prod, gath, mixb, mixbt, tw, aa, yacc, ff, cc, part, sbuf, rbuf, hs, hh, fs, fb,
    loc, s1s, s1r, ags, agr, hss, hsr, rss, rsr, s9s, s9r,
):
    d = lax.axis_index("seq")
    y = lax.axis_index("ch")
    x, z, c = d // 16, (d // 2) % NZ, d % 2

    def seq_of(xx, zz, c_):
        return 16 * xx + 2 * zz + c_

    loads = [
        pltpu.make_async_copy(key_in, key_v, loc.at[0]),
        pltpu.make_async_copy(value_in, value_v, loc.at[1]),
        pltpu.make_async_copy(mix_in.at[z], mix_s, loc.at[2]),
        pltpu.make_async_copy(mixt_in.at[z], mixt_s, loc.at[3]),
        pltpu.make_async_copy(twist_in.at[z], twist_s, loc.at[4]),
        pltpu.make_async_copy(spec_in, spec_v, loc.at[5]),
        pltpu.make_async_copy(cs_in, cs_v, loc.at[6]),
        pltpu.make_async_copy(gate_in, gate_v, loc.at[7]),
    ]
    loads[0].start()
    loads[1].start()

    xs = [lax.rem(x + i, NX) for i in range(NX)]
    cores = [c, 1 - c]
    plane = [(2 * xx + c_, seq_of(xx, z, c_)) for xx in xs for c_ in cores]

    def each_peer(act):
        for place, seq in plane[1:]:
            act(place, seq, y)

        def others(i, carry):
            yy = lax.rem(y + i, NY)
            for place, seq in plane:
                act(place, seq, yy)
            return carry

        lax.fori_loop(1, NY, others, 0)

    barrier = pltpu.get_barrier_semaphore()

    def greet(place, seq, yy):
        pl.semaphore_signal(barrier, inc=1, device_id={"seq": seq, "ch": yy}, device_id_type=MESH)

    each_peer(greet)
    up, down = seq_of(x, (z + 1) % NZ, c), seq_of(x, (z + NZ - 1) % NZ, c)
    for nb in (up, down):
        pl.semaphore_signal(barrier, inc=1, device_id={"seq": nb, "ch": y}, device_id_type=MESH)

    def wait_bytes(ref, sem):
        pltpu.make_async_copy(ref, ref, sem).wait()

    mine = 2 * x + c
    own = 8 * y + mine

    after = [lax.rem(y + k, NY) for k in range(NY)]
    before = [lax.rem(y + NY - k, NY) for k in range(NY)]

    def columns_of(yy, t):
        return pl.ds(pl.multiple_of(512 * yy + 128 * t, 128), LANES)

    def product_of(rows, cols):
        return (key_v[rows, cols].astype(f32) * value_v[rows, cols].astype(f32)).astype(bf16).astype(f32)

    def multiply(k):
        for t in range(4):
            cols = columns_of(before[k], t)
            pair = swap(product_of(pl.ds(0, 64), cols), product_of(pl.ds(64, 64), cols))
            for i in range(2):
                prod[8 * before[k] + 2 * t + i] = pair[i].astype(bf16)

    def spread_all(k):
        there = gath.at[k, z, mine]
        if k == 0:
            pltpu.make_async_copy(prod.at[own], there, s1r.at[k]).start()
        for place, seq in plane[k == 0 :]:
            pltpu.make_async_remote_copy(
                src_ref=prod.at[8 * before[k] + place],
                dst_ref=there,
                send_sem=s1s,
                recv_sem=s1r.at[k],
                device_id={"seq": seq, "ch": before[k]},
                device_id_type=MESH,
            ).start()

    def s1_wait(k):
        wait_bytes(gath.at[k, z], s1r.at[k])

    def one_hot(shape, axis):
        wide = lax.broadcasted_iota(jnp.int32, shape, axis) // 16
        return (wide == lax.broadcasted_iota(jnp.int32, shape, 1 - axis)).astype(f32).astype(bf16)

    def spread_table(small, big):
        rows, cols = small.shape[1], small.shape[2]
        diagonal = (lax.broadcasted_iota(jnp.int32, (16 * rows, 16 * cols), 0) % 16) == (
            lax.broadcasted_iota(jnp.int32, (16 * rows, 16 * cols), 1) % 16
        )
        for i in range(2):
            tall = dot(one_hot((16 * rows, rows), 0), small[i]).astype(bf16)
            wide = dot(tall, one_hot((cols, 16 * cols), 1))
            big[i] = jnp.where(diagonal, wide, 0.0).astype(bf16)

    def widen(k, carry):
        left = lax.broadcasted_iota(jnp.int32, (64, LANES), 1) < LANES // 2
        columns = [jnp.broadcast_to(twist_s[0, pl.ds(k + 16 * i, 1), :], (128, LANES)).T for i in range(2)]
        co, si = (jnp.where(left, a[:64], a[64:]) for a in columns)
        turns = [twist_s[1, pl.ds(k + 16 * i, 1), :] for i in range(2)]
        for v in range(4):
            t_co, t_si = (jnp.broadcast_to(a[:, v : v + 1], (64, LANES)) for a in turns)
            tw[k, v] = co * t_co - si * t_si
            tw[16 + k, v] = si * t_co + co * t_si
        return carry

    def repack(m, carry):
        rows = pl.ds(pl.multiple_of(16 * m, 16), 16)
        for t in range(4):
            for i in range(2):
                at = rows, pl.ds(128 * t, LANES)
                pair = swap(spec_v[(i, 0, *at)], spec_v[(i, 1, *at)])
                for k in range(2):
                    hs[2 * t + k, i, rows, :] = pair[k].astype(bf16)
        return carry

    def filter_send():
        pltpu.make_async_copy(hs.at[mine], hh.at[mine], hsr).start()
        for place, seq in plane[1:]:
            pltpu.make_async_remote_copy(
                src_ref=hs.at[place], dst_ref=hh.at[mine], send_sem=hss, recv_sem=hsr,
                device_id={"seq": seq, "ch": y}, device_id_type=MESH,
            ).start()

    def ag_copy(n, way, s, h):
        slot = (z - (s - 1)) % NZ if way == 0 else (z + (s - 1)) % NZ
        ref = gath.at[n, slot, pl.ds(4 * h, 4)]
        return pltpu.make_async_remote_copy(
            src_ref=ref, dst_ref=ref, send_sem=ags.at[n], recv_sem=agr.at[n, way, s - 1, h],
            device_id={"seq": up if way == 0 else down, "ch": y}, device_id_type=MESH,
        )

    def ag_wait(n, way, s, h):
        slot = (z - s) % NZ if way == 0 else (z + s) % NZ
        wait_bytes(gath.at[n, slot, pl.ds(4 * h, 4)], agr.at[n, way, s - 1, h])

    def ag_begin(n, h):
        for way in range(2):
            ag_copy(n, way, 1, h).start()

    def ag_step(n, s, h):
        for way in range(2):
            ag_wait(n, way, s, h)
            if s < 3 or h == way:
                ag_copy(n, way, s + 1, h).start()

    def ag_end(n):
        ag_wait(n, 0, 4, 0)
        ag_wait(n, 1, 4, 1)

    def mix(n):
        def body(v, carry):
            rows = [pl.ds(pl.multiple_of(32 * v + 16 * u, 16), 16) for u in range(2)]
            halves = [gath[n, :, :, rows[u], :].reshape(1024, LANES) for u in range(2)]
            data = jnp.concatenate(halves, axis=1)
            got = (dot(mixb[0], data) + dot(mixb[1], data)).reshape(8, 2, 2, 16, 2 * LANES)
            for u in range(2):
                lanes = slice(LANES * u, LANES * (u + 1))
                pairs = []
                for b in range(2):
                    re, im = got[:, b, 0, :, lanes], got[:, b, 1, :, lanes]
                    at = after[n], rows[u]
                    co = jnp.stack([tw[(2 * k + b, *at)] for k in range(8)])
                    si = jnp.stack([tw[(16 + 2 * k + b, *at)] for k in range(8)])
                    pairs.append((re * co + im * si, im * co - re * si))
                for i in range(2):
                    for jh, tile in enumerate(swap(pairs[0][i], pairs[1][i])):
                        aa[i, :, after[n], jh, rows[u], :] = tile.astype(bf16)
            return carry

        lax.fori_loop(0, 2, body, 0)

    def forward(g, w):
        both = after[2 * g : 2 * g + 2]
        re, im = (
            jnp.concatenate(
                [jnp.concatenate([aa[i, 2 * w + k, yy].reshape(128, LANES) for k in range(2)], axis=1) for yy in both], axis=0
            )
            for i in range(2)
        )
        y_re, y_im = (yacc[i, w] if g else 0.0 for i in range(2))
        for k in range(PASSES):
            co, si = (
                jnp.concatenate([cs_v[k, i, :, pl.ds(pl.multiple_of(128 * yy, 128), 128)] for yy in both], axis=1)
                for i in range(2)
            )
            y_re = y_re + (dot(co, re) + dot(si, im))
            y_im = y_im + (dot(co, im) - dot(si, re))
        if g == 0:
            yacc[0, w] = y_re
            yacc[1, w] = y_im
            return
        h_re, h_im = (
            jnp.concatenate([hh[2 * w + k, i] for k in range(2)], axis=1).astype(f32) for i in range(2)
        )
        ff[0, w] = (y_re * h_re - y_im * h_im).astype(bf16)
        ff[1, w] = (y_re * h_im + y_im * h_re).astype(bf16)

    def inverse(n):
        rows = pl.ds(pl.multiple_of(128 * after[n], 128), 128)
        tabs = [[cs_v[k, i, rows, :] for i in range(2)] for k in range(PASSES)]
        for w in range(4):
            re, im = ff[0, w], ff[1, w]
            g_re = g_im = 0.0
            for co, si in tabs:
                g_re = g_re + (dot(co, re) - dot(si, im))
                g_im = g_im + (dot(co, im) + dot(si, re))
            for k in range(2):
                lanes = slice(LANES * k, LANES * (k + 1))
                b_re = swap(g_re[:64, lanes], g_re[64:, lanes])
                b_im = swap(g_im[:64, lanes], g_im[64:, lanes])
                for b in range(2):
                    f = 4 * w + 2 * k + b
                    co = tw[f, after[n]]
                    si = tw[16 + f, after[n]]
                    cc[n, 2 * f] = (b_re[b] * co - b_im[b] * si).astype(bf16)
                    cc[n, 2 * f + 1] = (b_im[b] * co + b_re[b] * si).astype(bf16)

    def unmix(n):
        def body(v, carry):
            rows = [pl.ds(pl.multiple_of(32 * v + 16 * u, 16), 16) for u in range(2)]
            halves = [cc[n, :, rows[u], :].reshape(512, LANES) for u in range(2)]
            data = jnp.concatenate(halves, axis=1)
            got = (dot(mixbt[0], data) + dot(mixbt[1], data)).reshape(8, 8, 16, 2 * LANES)
            for u in range(2):
                part[n, :, :, rows[u], :] = got[:, :, :, LANES * u : LANES * (u + 1)]
            return carry

        lax.fori_loop(0, 2, body, 0)

    def rs_step(n, s, h):
        for way in range(2):
            if s == 1 and h != way:
                continue
            target = (z + 5 - s) % NZ if way == 0 else (z + 3 + s) % NZ
            piece = pl.ds(4 * h, 4)
            has = s > 2 or (s == 2 and h == way)
            total = part[n, target, piece]
            if has:
                wait_bytes(rbuf.at[n, way, s - 2, piece], rsr.at[n, way, s - 2, h])
                total = total + rbuf[n, way, s - 2, piece].astype(f32)
            sbuf[n, way, s - 1, piece] = total.astype(bf16)
            pltpu.make_async_remote_copy(
                src_ref=sbuf.at[n, way, s - 1, piece], dst_ref=rbuf.at[n, way, s - 1, piece],
                send_sem=rss.at[n], recv_sem=rsr.at[n, way, s - 1, h],
                device_id={"seq": up if way == 0 else down, "ch": y}, device_id_type=MESH,
            ).start()

    def rs_end(n):
        for h in range(2):
            piece = pl.ds(4 * h, 4)
            for way in range(2):
                wait_bytes(rbuf.at[n, way, 3, piece], rsr.at[n, way, 3, h])
            total = part[n, z, piece] + (rbuf[n, 0, 3, piece].astype(f32) + rbuf[n, 1, 3, piece].astype(f32))
            fs[n, piece] = total.astype(bf16)

    def give_all(k):
        if k == 0:
            pltpu.make_async_copy(fs.at[k, mine], fb.at[own], s9r.at[k]).start()
        for place, seq in plane[k == 0 :]:
            pltpu.make_async_remote_copy(
                src_ref=fs.at[k, place], dst_ref=fb.at[own], send_sem=s9s, recv_sem=s9r.at[k],
                device_id={"seq": seq, "ch": after[k]}, device_id_type=MESH,
            ).start()

    def finish(k):
        wait_bytes(fb.at[pl.ds(8 * before[k], 8)], s9r.at[k])
        for t in range(4):
            cols = columns_of(before[k], t)
            pair = swap(*(fb[8 * before[k] + 2 * t + i].astype(f32) for i in range(2)))
            for jh in range(2):
                rows = pl.ds(64 * jh, 64)
                field = pair[jh] + bias_ref[:, cols] * product_of(rows, cols)
                out_ref[rows, cols] = (gate_v[rows, cols].astype(f32) * field).astype(bf16)

    loads[0].wait()
    loads[1].wait()
    multiply(0)
    pl.semaphore_wait(barrier, 33)
    spread_all(0)
    multiply(1)
    spread_all(1)
    multiply(2)
    spread_all(2)
    multiply(3)
    spread_all(3)
    for load in loads[2:]:
        load.start()
    s1_wait(0)
    ag_begin(0, 0)
    ag_begin(0, 1)
    loads[5].wait()
    lax.fori_loop(0, 8, repack, 0)
    loads[4].wait()
    lax.fori_loop(0, 4, widen, 0)
    lax.fori_loop(8, 16, repack, 0)
    ag_step(0, 1, 0)
    lax.fori_loop(4, 8, widen, 0)
    s1_wait(1)
    ag_begin(1, 0)
    ag_begin(1, 1)
    ag_step(0, 1, 1)
    lax.fori_loop(16, 24, repack, 0)
    s1_wait(2)
    ag_begin(2, 0)
    ag_begin(2, 1)
    lax.fori_loop(8, 12, widen, 0)
    ag_step(0, 2, 0)
    loads[3].wait()
    spread_table(mixt_s, mixbt)
    ag_step(1, 1, 0)
    lax.fori_loop(24, 32, repack, 0)
    ag_step(1, 1, 1)
    s1_wait(3)
    ag_begin(3, 0)
    ag_begin(3, 1)
    filter_send()
    ag_step(0, 2, 1)
    lax.fori_loop(12, 16, widen, 0)
    ag_step(2, 1, 0)
    loads[2].wait()
    spread_table(mix_s, mixb)
    ag_step(2, 1, 1)
    ag_step(0, 3, 0)
    ag_step(1, 2, 0)
    ag_step(1, 2, 1)
    ag_step(3, 1, 0)
    ag_step(3, 1, 1)
    ag_step(0, 3, 1)
    ag_step(2, 2, 0)
    ag_step(2, 2, 1)
    ag_step(1, 3, 0)
    ag_step(1, 3, 1)
    ag_step(3, 2, 0)
    ag_step(3, 2, 1)
    ag_end(0)
    mix(0)
    ag_step(2, 3, 0)
    ag_step(2, 3, 1)
    ag_end(1)
    mix(1)
    ag_step(3, 3, 0)
    loads[6].wait()
    forward(0, 3)
    forward(0, 0)
    ag_step(3, 3, 1)
    forward(0, 2)
    forward(0, 1)
    ag_end(2)
    mix(2)
    ag_end(3)
    mix(3)
    wait_bytes(hh, hsr)
    forward(1, 0)
    forward(1, 3)
    forward(1, 1)
    forward(1, 2)
    inverse(0)
    unmix(0)
    rs_step(0, 1, 0)
    rs_step(0, 1, 1)
    inverse(1)
    unmix(1)
    rs_step(1, 1, 0)
    rs_step(0, 2, 0)
    rs_step(1, 1, 1)
    rs_step(0, 2, 1)
    inverse(2)
    unmix(2)
    rs_step(1, 2, 0)
    rs_step(0, 3, 0)
    rs_step(2, 1, 0)
    rs_step(1, 2, 1)
    rs_step(2, 1, 1)
    inverse(3)
    rs_step(0, 3, 1)
    unmix(3)
    rs_step(1, 3, 0)
    rs_step(0, 4, 0)
    rs_step(2, 2, 0)
    rs_step(3, 1, 0)
    rs_step(3, 1, 1)
    rs_step(1, 3, 1)
    rs_step(2, 2, 1)
    rs_step(0, 4, 1)
    rs_step(1, 4, 0)
    rs_step(2, 3, 0)
    rs_step(3, 2, 0)
    rs_step(3, 2, 1)
    rs_step(1, 4, 1)
    rs_step(2, 3, 1)
    rs_end(0)
    give_all(0)
    rs_step(2, 4, 0)
    rs_step(3, 3, 0)
    loads[7].wait()
    finish(0)
    rs_step(3, 3, 1)
    rs_end(1)
    give_all(1)
    rs_step(2, 4, 1)
    rs_step(3, 4, 0)
    finish(1)
    rs_step(3, 4, 1)
    rs_end(2)
    give_all(2)
    rs_end(3)
    give_all(3)
    finish(2)
    finish(3)

    wait_bytes(prod.at[pl.ds(0, 31)], s1s)
    wait_bytes(prod.at[pl.ds(0, 31)], s9s)
    wait_bytes(hs.at[pl.ds(0, 7)], hss)
    for n in range(4):
        wait_bytes(gath.at[n, pl.ds(0, 7)], ags.at[n])
        wait_bytes(gath.at[n, pl.ds(0, 7)], rss.at[n])


def per_device(gate_rows, key_rows, value_rows, spectrum, skip_bias):
    cs, mix, mix_t, twist = tables()
    anywhere = pl.BlockSpec(memory_space=pl.ANY)
    vmem = pl.BlockSpec(memory_space=pltpu.VMEM)
    rows, width = gate_rows.shape
    dma = pltpu.SemaphoreType.DMA
    return pl.pallas_call(
        kernel,
        out_shape=jax.ShapeDtypeStruct((rows, width), bf16),
        in_specs=[anywhere] * 8 + [vmem],
        out_specs=vmem,
        scratch_shapes=[
            pltpu.VMEM((rows, width), bf16),
            pltpu.VMEM((rows, width), bf16),
            pltpu.VMEM((rows, width), bf16),
            pltpu.VMEM((2, 2, 512, 512), f32),
            pltpu.VMEM((PASSES, 2, 512, 512), bf16),
            pltpu.VMEM((2, 32, 64), bf16),
            pltpu.VMEM((2, 64, 32), bf16),
            pltpu.VMEM((2, 32, 128), f32),
            pltpu.VMEM((32, 64, LANES), bf16),
            pltpu.VMEM((4, NZ, 8, 64, LANES), bf16),
            pltpu.VMEM((2, 512, 1024), bf16),
            pltpu.VMEM((2, 1024, 512), bf16),
            pltpu.VMEM((32, 4, 64, LANES), f32),
            pltpu.VMEM((2, 8, 4, 2, 64, LANES), bf16),
            pltpu.VMEM((2, 4, 512, 2 * LANES), f32),
            pltpu.VMEM((2, 4, 512, 2 * LANES), bf16),
            pltpu.VMEM((4, 32, 64, LANES), bf16),
            pltpu.VMEM((4, NZ, 8, 64, LANES), f32),
            pltpu.VMEM((4, 2, 4, 8, 64, LANES), bf16),
            pltpu.VMEM((4, 2, 4, 8, 64, LANES), bf16),
            pltpu.VMEM((8, 2, 512, LANES), bf16),
            pltpu.VMEM((8, 2, 512, LANES), bf16),
            pltpu.VMEM((4, 8, 64, LANES), bf16),
            pltpu.VMEM((32, 64, LANES), bf16),
            dma((8,)),
            dma, dma((4,)),
            dma((4,)), dma((4, 2, 4, 2)),
            dma, dma,
            dma((4,)), dma((4, 2, 4, 2)),
            dma, dma((4,)),
        ],
        compiler_params=pltpu.CompilerParams(
            collective_id=0, has_side_effects=True, vmem_limit_bytes=60 * 1024 * 1024
        ),
        name="hyena",
    )(gate_rows, key_rows, value_rows, spectrum, *(jnp.asarray(t) for t in (cs, mix, mix_t, twist)), skip_bias.reshape(1, width))


def solution(mesh):
    placed = (
        P(("seq", "ch"), None),
        P(("seq", "ch"), None),
        P(("seq", "ch"), None),
        P(None, "seq", None, "ch"),
        P(),
    )
    return jax.shard_map(
        per_device, mesh=mesh, in_specs=placed, out_specs=P(("seq", "ch"), None), check_vma=False
    )
```

```python
import math

import jax
import jax.numpy as jnp
import numpy as np
from jax import lax
from jax.experimental import pallas as pl
from jax.experimental.pallas import tpu as pltpu
from jax.sharding import PartitionSpec as P

f32, bf16 = jnp.float32, jnp.bfloat16
MESH = pl.DeviceIdType.MESH
NX, NZ, NC, NY = 4, 8, 2, 4
LANES = 128
PASSES = 1


def split(a):
    hi = a.astype(np.float32).astype(jnp.bfloat16)
    lo = (a - hi.astype(np.float64)).astype(np.float32).astype(jnp.bfloat16)
    return np.stack([hi, lo])


def tables():
    r = np.arange(512)
    turn = 2 * np.pi * (np.outer(r, r) % 512) / 512
    cs = np.stack([split(np.cos(turn))[:PASSES], split(np.sin(turn))[:PASSES]], 1)
    kx, kc, b = np.meshgrid(np.arange(4), np.arange(2), np.arange(2), indexing="ij")
    base = (32 * kx + 2 * kc + b).reshape(16)
    pz, px, pc = np.meshgrid(np.arange(8), np.arange(4), np.arange(2), indexing="ij")
    p = (16 * px + 2 * pz + pc).reshape(64)
    mix, mix_t, twist = [], [], []
    for z in range(8):
        k1 = base + 4 * z
        turn = 2 * np.pi * (np.outer(k1, p) % 128) / 128
        w = np.stack([np.cos(turn), -np.sin(turn)], 1).reshape(32, 64)
        mix.append(split(w))
        mix_t.append(split(w.T / 65536))
        both = []
        for r in (np.arange(128), 128 * (np.arange(128) % 4)):
            turn = 2 * np.pi * (np.outer(k1, r) % 65536) / 65536
            both.append(np.concatenate([np.cos(turn), np.sin(turn)]))
        twist.append(np.stack(both))
    return cs, np.stack(mix), np.stack(mix_t), np.stack(twist).astype(np.float32)


def dot(a, b):
    return jnp.dot(a, b, preferred_element_type=f32)


def swap(a, b):
    left = lax.broadcasted_iota(jnp.int32, a.shape, a.ndim - 1) < LANES // 2
    ra, rb = pltpu.roll(a, LANES // 2, a.ndim - 1), pltpu.roll(b, LANES // 2, a.ndim - 1)
    return jnp.where(left, a, rb), jnp.where(left, ra, b)


def kernel(
    gate_in, key_in, value_in, spec_in, cs_in, mix_in, mixt_in, twist_in, bias_ref, out_ref,
    gate_v, key_v, value_v, spec_v, cs_v, mix_s, mixt_s, twist_s,
    prod, gath, mixb, mixbt, tw, aa, yacc, ff, cc, part, sbuf, rbuf, hs, hh, fs, fb,
    loc, s1s, s1r, ags, agr, hss, hsr, rss, rsr, s9s, s9r,
):
    d = lax.axis_index("seq")
    y = lax.axis_index("ch")
    x, z, c = d // 16, (d // 2) % NZ, d % 2

    def seq_of(xx, zz, c_):
        return 16 * xx + 2 * zz + c_

    loads = [
        pltpu.make_async_copy(key_in, key_v, loc.at[0]),
        pltpu.make_async_copy(value_in, value_v, loc.at[1]),
        pltpu.make_async_copy(mix_in.at[z], mix_s, loc.at[2]),
        pltpu.make_async_copy(mixt_in.at[z], mixt_s, loc.at[3]),
        pltpu.make_async_copy(twist_in.at[z], twist_s, loc.at[4]),
        pltpu.make_async_copy(spec_in, spec_v, loc.at[5]),
        pltpu.make_async_copy(cs_in, cs_v, loc.at[6]),
        pltpu.make_async_copy(gate_in, gate_v, loc.at[7]),
    ]
    loads[0].start()
    loads[1].start()

    xs = [lax.rem(x + i, NX) for i in range(NX)]
    cores = [c, 1 - c]
    plane = [(2 * xx + c_, seq_of(xx, z, c_)) for xx in xs for c_ in cores]

    def each_peer(act):
        for place, seq in plane[1:]:
            act(place, seq, y)

        def others(i, carry):
            yy = lax.rem(y + i, NY)
            for place, seq in plane:
                act(place, seq, yy)
            return carry

        lax.fori_loop(1, NY, others, 0)

    barrier = pltpu.get_barrier_semaphore()

    def greet(place, seq, yy):
        pl.semaphore_signal(barrier, inc=1, device_id={"seq": seq, "ch": yy}, device_id_type=MESH)

    each_peer(greet)
    up, down = seq_of(x, (z + 1) % NZ, c), seq_of(x, (z + NZ - 1) % NZ, c)
    for nb in (up, down):
        pl.semaphore_signal(barrier, inc=1, device_id={"seq": nb, "ch": y}, device_id_type=MESH)

    def wait_bytes(ref, sem):
        pltpu.make_async_copy(ref, ref, sem).wait()

    mine = 2 * x + c
    own = 8 * y + mine

    after = [lax.rem(y + k, NY) for k in range(NY)]
    before = [lax.rem(y + NY - k, NY) for k in range(NY)]

    def columns_of(yy, t):
        return pl.ds(pl.multiple_of(512 * yy + 128 * t, 128), LANES)

    def product_of(rows, cols):
        return (key_v[rows, cols].astype(f32) * value_v[rows, cols].astype(f32)).astype(bf16).astype(f32)

    def multiply(k):
        for t in range(4):
            cols = columns_of(before[k], t)
            pair = swap(product_of(pl.ds(0, 64), cols), product_of(pl.ds(64, 64), cols))
            for i in range(2):
                prod[8 * before[k] + 2 * t + i] = pair[i].astype(bf16)

    def spread_all(k):
        there = gath.at[k, z, mine]
        if k == 0:
            pltpu.make_async_copy(prod.at[own], there, s1r.at[k]).start()
        for place, seq in plane[k == 0 :]:
            pltpu.make_async_remote_copy(
                src_ref=prod.at[8 * before[k] + place],
                dst_ref=there,
                send_sem=s1s,
                recv_sem=s1r.at[k],
                device_id={"seq": seq, "ch": before[k]},
                device_id_type=MESH,
            ).start()

    def s1_wait(k):
        wait_bytes(gath.at[k, z], s1r.at[k])

    def one_hot(shape, axis):
        wide = lax.broadcasted_iota(jnp.int32, shape, axis) // 16
        return (wide == lax.broadcasted_iota(jnp.int32, shape, 1 - axis)).astype(f32).astype(bf16)

    def spread_table(small, big):
        rows, cols = small.shape[1], small.shape[2]
        diagonal = (lax.broadcasted_iota(jnp.int32, (16 * rows, 16 * cols), 0) % 16) == (
            lax.broadcasted_iota(jnp.int32, (16 * rows, 16 * cols), 1) % 16
        )
        for i in range(2):
            tall = dot(one_hot((16 * rows, rows), 0), small[i]).astype(bf16)
            wide = dot(tall, one_hot((cols, 16 * cols), 1))
            big[i] = jnp.where(diagonal, wide, 0.0).astype(bf16)

    def widen(k, carry):
        left = lax.broadcasted_iota(jnp.int32, (64, LANES), 1) < LANES // 2
        columns = [jnp.broadcast_to(twist_s[0, pl.ds(k + 16 * i, 1), :], (128, LANES)).T for i in range(2)]
        co, si = (jnp.where(left, a[:64], a[64:]) for a in columns)
        turns = [twist_s[1, pl.ds(k + 16 * i, 1), :] for i in range(2)]
        for v in range(4):
            t_co, t_si = (jnp.broadcast_to(a[:, v : v + 1], (64, LANES)) for a in turns)
            tw[k, v] = co * t_co - si * t_si
            tw[16 + k, v] = si * t_co + co * t_si
        return carry

    def repack(m, carry):
        rows = pl.ds(pl.multiple_of(16 * m, 16), 16)
        for t in range(4):
            for i in range(2):
                at = rows, pl.ds(128 * t, LANES)
                pair = swap(spec_v[(i, 0, *at)], spec_v[(i, 1, *at)])
                for k in range(2):
                    hs[2 * t + k, i, rows, :] = pair[k].astype(bf16)
        return carry

    def filter_send():
        pltpu.make_async_copy(hs.at[mine], hh.at[mine], hsr).start()
        for place, seq in plane[1:]:
            pltpu.make_async_remote_copy(
                src_ref=hs.at[place], dst_ref=hh.at[mine], send_sem=hss, recv_sem=hsr,
                device_id={"seq": seq, "ch": y}, device_id_type=MESH,
            ).start()

    def ag_copy(n, way, s, h):
        slot = (z - (s - 1)) % NZ if way == 0 else (z + (s - 1)) % NZ
        ref = gath.at[n, slot, pl.ds(4 * h, 4)]
        return pltpu.make_async_remote_copy(
            src_ref=ref, dst_ref=ref, send_sem=ags.at[n], recv_sem=agr.at[n, way, s - 1, h],
            device_id={"seq": up if way == 0 else down, "ch": y}, device_id_type=MESH,
        )

    def ag_wait(n, way, s, h):
        slot = (z - s) % NZ if way == 0 else (z + s) % NZ
        wait_bytes(gath.at[n, slot, pl.ds(4 * h, 4)], agr.at[n, way, s - 1, h])

    def ag_begin(n, h):
        for way in range(2):
            ag_copy(n, way, 1, h).start()

    def ag_step(n, s, h):
        for way in range(2):
            ag_wait(n, way, s, h)
            if s < 3 or h == way:
                ag_copy(n, way, s + 1, h).start()

    def ag_end(n):
        ag_wait(n, 0, 4, 0)
        ag_wait(n, 1, 4, 1)

    def mix(n):
        def body(v, carry):
            rows = [pl.ds(pl.multiple_of(32 * v + 16 * u, 16), 16) for u in range(2)]
            halves = [gath[n, :, :, rows[u], :].reshape(1024, LANES) for u in range(2)]
            data = jnp.concatenate(halves, axis=1)
            got = (dot(mixb[0], data) + dot(mixb[1], data)).reshape(8, 2, 2, 16, 2 * LANES)
            for u in range(2):
                lanes = slice(LANES * u, LANES * (u + 1))
                pairs = []
                for b in range(2):
                    re, im = got[:, b, 0, :, lanes], got[:, b, 1, :, lanes]
                    at = after[n], rows[u]
                    co = jnp.stack([tw[(2 * k + b, *at)] for k in range(8)])
                    si = jnp.stack([tw[(16 + 2 * k + b, *at)] for k in range(8)])
                    pairs.append((re * co + im * si, im * co - re * si))
                for i in range(2):
                    for jh, tile in enumerate(swap(pairs[0][i], pairs[1][i])):
                        aa[i, :, after[n], jh, rows[u], :] = tile.astype(bf16)
            return carry

        lax.fori_loop(0, 2, body, 0)

    def forward(g, w):
        both = after[2 * g : 2 * g + 2]
        re, im = (
            jnp.concatenate(
                [jnp.concatenate([aa[i, 2 * w + k, yy].reshape(128, LANES) for k in range(2)], axis=1) for yy in both], axis=0
            )
            for i in range(2)
        )
        y_re, y_im = (yacc[i, w] if g else 0.0 for i in range(2))
        for k in range(PASSES):
            co, si = (
                jnp.concatenate([cs_v[k, i, :, pl.ds(pl.multiple_of(128 * yy, 128), 128)] for yy in both], axis=1)
                for i in range(2)
            )
            y_re = y_re + (dot(co, re) + dot(si, im))
            y_im = y_im + (dot(co, im) - dot(si, re))
        if g == 0:
            yacc[0, w] = y_re
            yacc[1, w] = y_im
            return
        h_re, h_im = (
            jnp.concatenate([hh[2 * w + k, i] for k in range(2)], axis=1).astype(f32) for i in range(2)
        )
        ff[0, w] = (y_re * h_re - y_im * h_im).astype(bf16)
        ff[1, w] = (y_re * h_im + y_im * h_re).astype(bf16)

    def inverse(n):
        rows = pl.ds(pl.multiple_of(128 * after[n], 128), 128)
        tabs = [[cs_v[k, i, rows, :] for i in range(2)] for k in range(PASSES)]
        for w in range(4):
            re, im = ff[0, w], ff[1, w]
            g_re = g_im = 0.0
            for co, si in tabs:
                g_re = g_re + (dot(co, re) - dot(si, im))
                g_im = g_im + (dot(co, im) + dot(si, re))
            for k in range(2):
                lanes = slice(LANES * k, LANES * (k + 1))
                b_re = swap(g_re[:64, lanes], g_re[64:, lanes])
                b_im = swap(g_im[:64, lanes], g_im[64:, lanes])
                for b in range(2):
                    f = 4 * w + 2 * k + b
                    co = tw[f, after[n]]
                    si = tw[16 + f, after[n]]
                    cc[n, 2 * f] = (b_re[b] * co - b_im[b] * si).astype(bf16)
                    cc[n, 2 * f + 1] = (b_im[b] * co + b_re[b] * si).astype(bf16)

    def unmix(n):
        def body(v, carry):
            rows = [pl.ds(pl.multiple_of(32 * v + 16 * u, 16), 16) for u in range(2)]
            halves = [cc[n, :, rows[u], :].reshape(512, LANES) for u in range(2)]
            data = jnp.concatenate(halves, axis=1)
            got = (dot(mixbt[0], data) + dot(mixbt[1], data)).reshape(8, 8, 16, 2 * LANES)
            for u in range(2):
                part[n, :, :, rows[u], :] = got[:, :, :, LANES * u : LANES * (u + 1)]
            return carry

        lax.fori_loop(0, 2, body, 0)

    def unmix_first(n):
        far = lax.rem(z + NZ // 2, NZ)
        at = pl.ds(pl.multiple_of(128 * far, 128), 128)

        def body(v, carry):
            rows = [pl.ds(pl.multiple_of(32 * v + 16 * u, 16), 16) for u in range(2)]
            data = jnp.concatenate([cc[n, :, rows[u], :].reshape(512, LANES) for u in range(2)], axis=1)
            got = (dot(mixbt[0, at, :], data) + dot(mixbt[1, at, :], data)).reshape(8, 16, 2 * LANES)
            for u in range(2):
                part[n, far, :, rows[u], :] = got[:, :, LANES * u : LANES * (u + 1)]
            return carry

        lax.fori_loop(0, 2, body, 0)

    def rs_step(n, s, h):
        for way in range(2):
            if s == 1 and h != way:
                continue
            target = (z + 5 - s) % NZ if way == 0 else (z + 3 + s) % NZ
            piece = pl.ds(4 * h, 4)
            has = s > 2 or (s == 2 and h == way)
            total = part[n, target, piece]
            if has:
                wait_bytes(rbuf.at[n, way, s - 2, piece], rsr.at[n, way, s - 2, h])
                total = total + rbuf[n, way, s - 2, piece].astype(f32)
            sbuf[n, way, s - 1, piece] = total.astype(bf16)
            pltpu.make_async_remote_copy(
                src_ref=sbuf.at[n, way, s - 1, piece], dst_ref=rbuf.at[n, way, s - 1, piece],
                send_sem=rss.at[n], recv_sem=rsr.at[n, way, s - 1, h],
                device_id={"seq": up if way == 0 else down, "ch": y}, device_id_type=MESH,
            ).start()

    def rs_end(n):
        for h in range(2):
            piece = pl.ds(4 * h, 4)
            for way in range(2):
                wait_bytes(rbuf.at[n, way, 3, piece], rsr.at[n, way, 3, h])
            total = part[n, z, piece] + (rbuf[n, 0, 3, piece].astype(f32) + rbuf[n, 1, 3, piece].astype(f32))
            fs[n, piece] = total.astype(bf16)

    def give_all(k):
        if k == 0:
            pltpu.make_async_copy(fs.at[k, mine], fb.at[own], s9r.at[k]).start()
        for place, seq in plane[k == 0 :]:
            pltpu.make_async_remote_copy(
                src_ref=fs.at[k, place], dst_ref=fb.at[own], send_sem=s9s, recv_sem=s9r.at[k],
                device_id={"seq": seq, "ch": after[k]}, device_id_type=MESH,
            ).start()

    def finish(k):
        wait_bytes(fb.at[pl.ds(8 * before[k], 8)], s9r.at[k])
        for t in range(4):
            cols = columns_of(before[k], t)
            pair = swap(*(fb[8 * before[k] + 2 * t + i].astype(f32) for i in range(2)))
            for jh in range(2):
                rows = pl.ds(64 * jh, 64)
                field = pair[jh] + bias_ref[:, cols] * product_of(rows, cols)
                out_ref[rows, cols] = (gate_v[rows, cols].astype(f32) * field).astype(bf16)

    loads[0].wait()
    loads[1].wait()
    multiply(0)
    pl.semaphore_wait(barrier, 33)
    spread_all(0)
    multiply(1)
    spread_all(1)
    multiply(2)
    spread_all(2)
    multiply(3)
    spread_all(3)
    for load in loads[2:]:
        load.start()
    s1_wait(0)
    ag_begin(0, 0)
    ag_begin(0, 1)
    loads[5].wait()
    lax.fori_loop(0, 8, repack, 0)
    loads[4].wait()
    lax.fori_loop(0, 4, widen, 0)
    lax.fori_loop(8, 16, repack, 0)
    ag_step(0, 1, 0)
    lax.fori_loop(4, 8, widen, 0)
    s1_wait(1)
    ag_begin(1, 0)
    ag_begin(1, 1)
    ag_step(0, 1, 1)
    lax.fori_loop(16, 24, repack, 0)
    s1_wait(2)
    ag_begin(2, 0)
    ag_begin(2, 1)
    lax.fori_loop(8, 12, widen, 0)
    ag_step(0, 2, 0)
    loads[3].wait()
    spread_table(mixt_s, mixbt)
    ag_step(1, 1, 0)
    lax.fori_loop(24, 32, repack, 0)
    ag_step(1, 1, 1)
    s1_wait(3)
    ag_begin(3, 0)
    ag_begin(3, 1)
    filter_send()
    ag_step(0, 2, 1)
    lax.fori_loop(12, 16, widen, 0)
    ag_step(2, 1, 0)
    loads[2].wait()
    spread_table(mix_s, mixb)
    ag_step(2, 1, 1)
    ag_step(0, 3, 0)
    ag_step(1, 2, 0)
    ag_step(1, 2, 1)
    ag_step(3, 1, 0)
    ag_step(3, 1, 1)
    ag_step(0, 3, 1)
    ag_step(2, 2, 0)
    ag_step(2, 2, 1)
    ag_step(1, 3, 0)
    ag_step(1, 3, 1)
    ag_step(3, 2, 0)
    ag_step(3, 2, 1)
    ag_end(0)
    mix(0)
    ag_step(2, 3, 0)
    ag_step(2, 3, 1)
    ag_end(1)
    mix(1)
    ag_step(3, 3, 0)
    loads[6].wait()
    forward(0, 3)
    forward(0, 0)
    ag_step(3, 3, 1)
    forward(0, 2)
    forward(0, 1)
    ag_end(2)
    mix(2)
    ag_end(3)
    mix(3)
    wait_bytes(hh, hsr)
    forward(1, 0)
    forward(1, 3)
    forward(1, 1)
    forward(1, 2)
    inverse(0)
    unmix_first(0)
    rs_step(0, 1, 0)
    rs_step(0, 1, 1)
    unmix(0)
    inverse(1)
    unmix(1)
    rs_step(1, 1, 0)
    rs_step(0, 2, 0)
    rs_step(1, 1, 1)
    rs_step(0, 2, 1)
    inverse(2)
    unmix(2)
    rs_step(1, 2, 0)
    rs_step(0, 3, 0)
    rs_step(2, 1, 0)
    rs_step(1, 2, 1)
    rs_step(2, 1, 1)
    inverse(3)
    rs_step(0, 3, 1)
    unmix(3)
    rs_step(1, 3, 0)
    rs_step(0, 4, 0)
    rs_step(2, 2, 0)
    rs_step(3, 1, 0)
    rs_step(3, 1, 1)
    rs_step(1, 3, 1)
    rs_step(2, 2, 1)
    rs_step(0, 4, 1)
    rs_step(1, 4, 0)
    rs_step(2, 3, 0)
    rs_step(3, 2, 0)
    rs_step(3, 2, 1)
    rs_step(1, 4, 1)
    rs_step(2, 3, 1)
    rs_end(0)
    give_all(0)
    rs_step(2, 4, 0)
    rs_step(3, 3, 0)
    loads[7].wait()
    finish(0)
    rs_step(3, 3, 1)
    rs_end(1)
    give_all(1)
    rs_step(2, 4, 1)
    rs_step(3, 4, 0)
    finish(1)
    rs_step(3, 4, 1)
    rs_end(2)
    give_all(2)
    rs_end(3)
    give_all(3)
    finish(2)
    finish(3)

    wait_bytes(prod.at[pl.ds(0, 31)], s1s)
    wait_bytes(prod.at[pl.ds(0, 31)], s9s)
    wait_bytes(hs.at[pl.ds(0, 7)], hss)
    for n in range(4):
        wait_bytes(gath.at[n, pl.ds(0, 7)], ags.at[n])
        wait_bytes(gath.at[n, pl.ds(0, 7)], rss.at[n])


def per_device(gate_rows, key_rows, value_rows, spectrum, skip_bias):
    cs, mix, mix_t, twist = tables()
    anywhere = pl.BlockSpec(memory_space=pl.ANY)
    vmem = pl.BlockSpec(memory_space=pltpu.VMEM)
    rows, width = gate_rows.shape
    dma = pltpu.SemaphoreType.DMA
    return pl.pallas_call(
        kernel,
        out_shape=jax.ShapeDtypeStruct((rows, width), bf16),
        in_specs=[anywhere] * 8 + [vmem],
        out_specs=vmem,
        scratch_shapes=[
            pltpu.VMEM((rows, width), bf16),
            pltpu.VMEM((rows, width), bf16),
            pltpu.VMEM((rows, width), bf16),
            pltpu.VMEM((2, 2, 512, 512), f32),
            pltpu.VMEM((PASSES, 2, 512, 512), bf16),
            pltpu.VMEM((2, 32, 64), bf16),
            pltpu.VMEM((2, 64, 32), bf16),
            pltpu.VMEM((2, 32, 128), f32),
            pltpu.VMEM((32, 64, LANES), bf16),
            pltpu.VMEM((4, NZ, 8, 64, LANES), bf16),
            pltpu.VMEM((2, 512, 1024), bf16),
            pltpu.VMEM((2, 1024, 512), bf16),
            pltpu.VMEM((32, 4, 64, LANES), f32),
            pltpu.VMEM((2, 8, 4, 2, 64, LANES), bf16),
            pltpu.VMEM((2, 4, 512, 2 * LANES), f32),
            pltpu.VMEM((2, 4, 512, 2 * LANES), bf16),
            pltpu.VMEM((4, 32, 64, LANES), bf16),
            pltpu.VMEM((4, NZ, 8, 64, LANES), f32),
            pltpu.VMEM((4, 2, 4, 8, 64, LANES), bf16),
            pltpu.VMEM((4, 2, 4, 8, 64, LANES), bf16),
            pltpu.VMEM((8, 2, 512, LANES), bf16),
            pltpu.VMEM((8, 2, 512, LANES), bf16),
            pltpu.VMEM((4, 8, 64, LANES), bf16),
            pltpu.VMEM((32, 64, LANES), bf16),
            dma((8,)),
            dma, dma((4,)),
            dma((4,)), dma((4, 2, 4, 2)),
            dma, dma,
            dma((4,)), dma((4, 2, 4, 2)),
            dma, dma((4,)),
        ],
        compiler_params=pltpu.CompilerParams(
            collective_id=0, has_side_effects=True, vmem_limit_bytes=60 * 1024 * 1024
        ),
        name="hyena",
    )(gate_rows, key_rows, value_rows, spectrum, *(jnp.asarray(t) for t in (cs, mix, mix_t, twist)), skip_bias.reshape(1, width))


def solution(mesh):
    placed = (
        P(("seq", "ch"), None),
        P(("seq", "ch"), None),
        P(("seq", "ch"), None),
        P(None, "seq", None, "ch"),
        P(),
    )
    return jax.shard_map(
        per_device, mesh=mesh, in_specs=placed, out_specs=P(("seq", "ch"), None), check_vma=False
    )
```
